128 devices in a mesh: aux: 8 (over x, core), orb: 16 (over y, z).
Axes of the slice: x: 4, y: 4, z: 4, core: 2. Of those that a mesh axis runs over, the one named last changes fastest.
Arguments:
- raw_ints: bfloat16 [8, 16, 1024, 1536], P(None, 'orb', 'aux'), may hold values from -0.625 to 0.625
- fit_inverse: bfloat16 [128, 1024, 1024], P(('aux', 'orb')), may hold values from -0.1875 to 0.1875
- pair_orbs: int32 [2048, 2], P(('aux', 'orb')), may hold values from 0 to 15, all different within a row; in each aligned block of 16 rows (0 to 15, 16 to 31, ...) at most 4 rows name the same one
- pno_coef: bfloat16 [2048, 2, 32, 1536], P(('aux', 'orb')), may hold values from -0.15625 to 0.15625
- pno_energy: float32 [2048, 2, 32], P(('aux', 'orb')), may hold values from 0.3 to 6
- occ_energy: float32 [128], replicated, may hold values from -1.5 to -0.3
- fit_offset: int32 [128], replicated, may hold values from 0 to 255
Outputs:
- amplitude: float32 [2048, 1024], P(('aux', 'orb'))
- energy: float32 [2048], P(('aux', 'orb'))
The draws below stay inside these ranges and needn't reach their ends.
Inputs may be any that keep to these rules, and one draw needn't show every extreme that they name: `pair_orbs`: each entry is an orbital's index within the pair's region; the two entries of a row differ; among the rows of one device no orbital is named more than 4 times.
All inputs are finite; a program needn't handle non-finite values.
Results may differ from the reference program's by a relative error of at most 0.0057.
Values may be sent and summed in bfloat16 or wider, within the bound.
A program may use at most 64 MiB of HBM per device.

```python
import math
import jax
import jax.numpy as jnp
import numpy as np
from jax import lax

FIT = 1024
DOM = 1536
NPNO = 32
PAIR_DEV = 16
NREG = 8
NPER = 16
NORB = 128
NPAIR = 2048
CAP = 4


def place_ends(drawn, rng, least, top_value):
    extent = drawn.shape
    place = [jax.random.randint(jax.random.fold_in(rng, axis), (), 0, extent[axis]) for axis in range(len(extent))]
    drawn = drawn.at[tuple(place)].set(least)
    longest = extent.index(max(extent))
    place[longest] = (place[longest] + 1) % extent[longest]
    return drawn.at[tuple(place)].set(top_value)


def block_scale(rng, dims, shards, smallest, largest):
    def one(axis_at, blocks):
        draws = jax.random.uniform(jax.random.fold_in(jax.random.fold_in(rng, 6), axis_at), (blocks,), jnp.float32, smallest / len(shards), largest / len(shards))
        return jnp.repeat(jnp.exp(draws), dims[axis_at] // blocks).reshape((-1,) + (1,) * (len(dims) - axis_at - 1))

    level = one(*shards[0])
    for cut in shards[1:]:
        level = level * one(*cut)
    return level


def deal_out(rng, own, number, rows, number_of, top, reach, skew):
    sequence = jax.random.permutation(rng, number_of)
    packed, usual = shares(number_of, rows * top, reach, skew, True), shares(number_of, rows * top, reach, skew, False)
    places = jnp.arange(number_of)

    def named(tallies, rotation):
        used = int((tallies > 0).sum())
        fixed = max(1, used // 4)
        passed = fixed + (places - fixed + rotation * (used - fixed)) % max(1, number_of - fixed)
        return jnp.zeros((number_of,), jnp.int32).at[sequence[jnp.where(places < fixed, places, passed)]].set(jnp.asarray(tallies, jnp.int32))

    tallies = jnp.where(number % 4 == 0, named(packed, number // 4), named(usual, number - number // 4 - 1))
    mixed = jax.random.permutation(jax.random.fold_in(own, 3), number_of)
    giver, taker = mixed[0:number_of // 2 * 2:2], mixed[1:number_of // 2 * 2:2]
    room = jnp.minimum(tallies[giver] - 1, reach - tallies[taker]) // 2
    room = jnp.where((giver == sequence[0]) | (taker == sequence[0]) | (tallies[taker] == 0), 0, jnp.maximum(room, 0))
    passed = jax.random.randint(jax.random.fold_in(own, 4), (number_of // 2,), 0, 1 << 20) % (room + 1)
    tallies = tallies.at[giver].add(-passed).at[taker].add(passed)
    items = jnp.searchsorted(jnp.cumsum(tallies), jnp.arange(rows * top), side="right").astype(jnp.int32)
    grid = items.reshape(top, rows).T
    grid = grid[jax.random.permutation(jax.random.fold_in(own, 1), rows)]
    rotation = jax.random.randint(jax.random.fold_in(own, 2), (rows, 1), 0, top)
    return jnp.take_along_axis(grid, (jnp.arange(top)[None, :] + rotation) % top, axis=1)


def shares(number_of, total, limit, slope, full):
    weights = [(1 << 20) // math.isqrt(rank ** slope) + 1 for rank in range(1, number_of + 1)]
    largest = limit if full else min(limit, max(-(-total // number_of), total * weights[0] // sum(weights)))
    least = 1 if total - largest >= number_of - 1 else 0
    given, spare = [largest] + [least] * (number_of - 1), total - largest - least * (number_of - 1)
    while spare > 0:
        candidates = [i for i in range(1, number_of) if given[i] < largest] or [i for i in range(1, number_of) if given[i] < limit]
        mass, left = sum([weights[i] for i in candidates]), spare
        for i in candidates:
            more = min(limit - given[i], max(1, left * weights[i] // mass), spare)
            given[i] = given[i] + more
            spare = spare - more
    return np.array(given)


def scatter_about(key, dims, scale, bound, cuts=(), kind=jnp.bfloat16):
    array = scale * jax.random.normal(key, dims, jnp.float32)
    if cuts:
        array = array * block_scale(key, dims, cuts, -0.22, 0.18)
    return jnp.clip(array, -bound, bound).astype(kind)


def setup_inputs(seed: int = 0) -> dict:
    arg_keys = jax.random.split(jax.random.key(seed), 8)
    raw_ints = scatter_about(arg_keys[0], (NREG, NPER, FIT, DOM), 0.1, 0.625, ((1, 16), (2, 8)))
    fit_inverse = scatter_about(arg_keys[1], (NORB, FIT, FIT), FIT ** -0.5, 0.1875, ((0, 128),))
    pair_orbs_keys = jax.random.split(jax.random.fold_in(arg_keys[2], 1), NPAIR // PAIR_DEV)
    pair_orbs_turns = jax.random.permutation(jax.random.fold_in(arg_keys[2], 3), NPAIR // PAIR_DEV)
    pair_orbs = jax.vmap(lambda own, number: deal_out(jax.random.fold_in(arg_keys[2], 2), own, number, PAIR_DEV, NPER, 2, CAP, 2))(pair_orbs_keys, pair_orbs_turns).reshape((NPAIR, 2))
    pno_coef = scatter_about(arg_keys[3], (NPAIR, 2, NPNO, DOM), DOM ** -0.5, 0.15625, ((0, 128),))
    pno_energy = jnp.clip(jnp.exp(math.log(6.0) - 2.9957322 * jax.random.uniform(arg_keys[4], (NPAIR, 2, NPNO), jnp.float32) ** block_scale(arg_keys[4], (NPAIR, 2, NPNO), ((0, 128),), -0.2, 0.2)), 0.3, 6.0)
    occ_energy = jnp.clip(jax.random.uniform(arg_keys[5], (NORB,), jnp.float32, -1.5, -0.3), -1.5, -0.3)
    fit_offset = place_ends(jax.random.randint(arg_keys[6], (NORB,), 0, FIT // 4), jax.random.fold_in(arg_keys[6], 1), 0, (FIT // 4) - 1).astype(jnp.int32)
    return {"raw_ints": raw_ints, "fit_inverse": fit_inverse, "pair_orbs": pair_orbs, "pno_coef": pno_coef, "pno_energy": pno_energy, "occ_energy": occ_energy, "fit_offset": fit_offset}


def fit_block(operands):
    inverse, raw_block = operands
    return jnp.dot(inverse, raw_block, preferred_element_type=jnp.float32).astype(jnp.bfloat16)


def reference(raw_ints, fit_inverse, pair_orbs, pno_coef, pno_energy, occ_energy, fit_offset):
    blocks = raw_ints.reshape(NORB, FIT, DOM)
    fitted = lax.map(fit_block, (fit_inverse, blocks))
    region = jnp.arange(NPAIR, dtype=jnp.int32) // (PAIR_DEV * NPER)
    global_orb = (region[:, None] * NPER + pair_orbs).astype(jnp.int32)
    margin = FIT // 4
    contract = (((1,), (1,)), ((), ()))

    def one_pair(operands):
        orbitals, coef_pair, levels = operands
        first_side = lax.dot_general(coef_pair[0], fitted[orbitals[0]], contract, preferred_element_type=jnp.float32).astype(jnp.bfloat16)
        second = lax.dot_general(coef_pair[1], fitted[orbitals[1]], contract, preferred_element_type=jnp.float32).astype(jnp.bfloat16)
        shift_rows = (fit_offset[orbitals[0]] - fit_offset[orbitals[1]]).astype(jnp.int32)
        padded = jnp.pad(second, ((0, 0), (margin, margin)))
        aligned = lax.dynamic_slice_in_dim(padded, (margin + shift_rows).astype(jnp.int32), FIT, 1)
        coupling = lax.dot_general(first_side, aligned, contract, preferred_element_type=jnp.float32)
        denominator = levels[0][:, None] + levels[1][None, :] - occ_energy[orbitals[0]] - occ_energy[orbitals[1]]
        amplitude = -coupling / denominator
        energy = jnp.sum(coupling * (2.0 * amplitude - amplitude.T))
        return amplitude.reshape(NPNO * NPNO), energy

    amplitude, energy = lax.map(one_pair, (global_orb, pno_coef, pno_energy))
    return amplitude, energy
```

```python
import functools

import jax
import jax.numpy as jnp
from jax import lax
from jax.experimental import pallas as pl
from jax.experimental.pallas import tpu as pltpu
from jax.sharding import PartitionSpec as P

MESH = pl.DeviceIdType.MESH
HOPS = (1, 3, 2)
CAP = 4
LAG = 3


def exchange_kernel(
    side_of_slot, slot_of_side, offsets, raw_ref, inv_ref, coef_ref, out_ref,
    coef, inverse, rolled, gathered, fitted_t, away, mid, last, sides, back, home,
    left, right,
    local_sem, raw_send, raw_recv, p1_send, p1_recv, p2_send, p2_recv,
    r1_send, r1_recv, r2_send, r2_recv,
):
    aux = lax.axis_index("aux")
    orb = lax.axis_index("orb")
    x, core = aux // 2, lax.rem(aux, 2)
    y, z = orb // 4, lax.rem(orb, 4)
    fit = inverse.shape[0]
    dom = fitted_t.shape[0]
    npno = coef.shape[1]
    rows = raw_ref.shape[2]

    def turned(d_first, d_second):
        dy = jnp.where(core == 0, d_first, d_second)
        dz = jnp.where(core == 0, d_second, d_first)
        return lax.rem(y + dy, 4) * 4 + lax.rem(z + dz, 4)

    def raw_peer(dx, dc):
        return lax.rem(x + dx, 4) * 2 + lax.rem(core + dc, 2)

    load_coef = pltpu.make_async_copy(coef_ref, coef, local_sem.at[0])
    load_inverse = pltpu.make_async_copy(inv_ref.at[0], inverse, local_sem.at[1])
    load_own = pltpu.make_async_copy(
        raw_ref.at[aux, 0], gathered.at[pl.ds(aux * rows, rows)], local_sem.at[2]
    )
    load_coef.start()
    load_inverse.start()
    load_own.start()

    raw_hops = [(0, 1), (1, 0), (3, 0), (1, 1), (3, 1), (2, 0), (2, 1)]
    barrier = pltpu.get_barrier_semaphore()
    for d in HOPS:
        pl.semaphore_signal(barrier, 1, device_id=(aux, turned(d, 0)), device_id_type=MESH)
        pl.semaphore_signal(barrier, 1, device_id=(aux, turned(0, d)), device_id_type=MESH)
    for hop in raw_hops:
        pl.semaphore_signal(barrier, 1, device_id=(raw_peer(*hop), orb), device_id_type=MESH)
    pl.semaphore_wait(barrier, 2 * len(HOPS) + len(raw_hops))

    raw_copies = []
    for i, hop in enumerate(raw_hops):
        peer = raw_peer(*hop)
        raw_copies.append(
            pltpu.make_async_remote_copy(
                src_ref=raw_ref.at[peer, 0],
                dst_ref=gathered.at[pl.ds(aux * rows, rows)],
                send_sem=raw_send.at[i],
                recv_sem=raw_recv.at[i],
                device_id=(peer, orb),
                device_id_type=MESH,
            )
        )
        raw_copies[-1].start()

    def stage(da, db):
        base = turned(da, db) * CAP
        for j in range(CAP):
            away[da, db, j] = coef[side_of_slot[base + j]]

    first, second, third, fourth = {}, {}, {}, {}

    def send_first(da, db):
        k = (da - 1) * 4 + db
        first[da, db] = pltpu.make_async_remote_copy(
            src_ref=away.at[da, db], dst_ref=mid.at[da - 1, db],
            send_sem=p1_send.at[k], recv_sem=p1_recv.at[k],
            device_id=(aux, turned(da, 0)), device_id_type=MESH,
        )
        first[da, db].start()

    def send_second(da, db):
        k = da * 3 + db - 1
        source = away.at[0, db] if da == 0 else mid.at[da - 1, db]
        second[da, db] = pltpu.make_async_remote_copy(
            src_ref=source, dst_ref=last.at[da, db - 1],
            send_sem=p2_send.at[k], recv_sem=p2_recv.at[k],
            device_id=(aux, turned(0, db)), device_id_type=MESH,
        )
        second[da, db].start()

    def send_third(da, db):
        k = da * 3 + db - 1
        target = home.at[0, db] if da == 0 else back.at[da - 1, db - 1]
        third[da, db] = pltpu.make_async_remote_copy(
            src_ref=sides.at[da, db], dst_ref=target,
            send_sem=r1_send.at[k], recv_sem=r1_recv.at[k],
            device_id=(aux, turned(0, 4 - db)), device_id_type=MESH,
        )
        third[da, db].start()

    def send_fourth(da, db):
        k = (da - 1) * 4 + db
        source = sides.at[da, 0] if db == 0 else back.at[da - 1, db - 1]
        fourth[da, db] = pltpu.make_async_remote_copy(
            src_ref=source, dst_ref=home.at[da, db],
            send_sem=r2_send.at[k], recv_sem=r2_recv.at[k],
            device_id=(aux, turned(4 - da, 0)), device_id_type=MESH,
        )
        fourth[da, db].start()

    load_coef.wait()
    for db in (1, 3, 2, 0):
        for da in HOPS:
            stage(da, db)
            send_first(da, db)
        if db != 0:
            stage(0, db)
            send_second(0, db)
    stage(0, 0)

    load_inverse.wait()
    own_offset = offsets[aux * 16 + orb]
    tile = 256

    def turn(n, carry):
        start = pl.multiple_of(n * tile, tile)
        to_row = lax.broadcasted_iota(jnp.int32, (tile, fit), 0) + start
        from_row = lax.broadcasted_iota(jnp.int32, (tile, fit), 1)
        hit = jnp.bitwise_and(to_row - from_row - own_offset + 2 * fit, fit - 1) == 0
        pick = jnp.where(hit, 1.0, 0.0).astype(jnp.bfloat16)
        rolled[pl.ds(start, tile), :] = jnp.dot(
            pick, inverse[...], preferred_element_type=jnp.float32
        ).astype(jnp.bfloat16)
        return carry

    lax.fori_loop(0, fit // tile, turn, 0)

    for db in HOPS:
        for da in HOPS:
            first[da, db].wait_recv()
            send_second(da, db)
    for da in HOPS:
        first[da, 0].wait_recv()

    load_own.wait()
    for copy in raw_copies:
        copy.wait_recv()

    def fit_tile(n, carry):
        start = pl.multiple_of(n * tile, tile)
        block = jnp.dot(
            rolled[...], gathered[:, pl.ds(start, tile)], preferred_element_type=jnp.float32
        ).astype(jnp.bfloat16)
        fitted_t[pl.ds(start, tile), :] = block.T
        return carry

    lax.fori_loop(0, dom // tile, fit_tile, 0)

    def project(source, target):
        def columns(n, carry):
            start = pl.multiple_of(n * tile, tile)
            lhs = source[...].reshape(CAP * npno, dom)
            block = jnp.dot(
                lhs, fitted_t[:, pl.ds(start, tile)], preferred_element_type=jnp.float32
            ).astype(jnp.bfloat16)
            target[:, :, pl.ds(start, tile)] = block.reshape(CAP, npno, tile)
            return carry

        lax.fori_loop(0, fit // tile, columns, 0)

    for da in HOPS:
        project(mid.at[da - 1, 0], sides.at[da, 0])
        send_fourth(da, 0)
    project(away.at[0, 0], home.at[0, 0])
    order = [(0, db) for db in HOPS] + [(da, db) for db in HOPS for da in HOPS]
    for i, (da, db) in enumerate(order):
        second[da, db].wait_recv()
        project(last.at[da, db - 1], sides.at[da, db])
        send_third(da, db)
        if i >= LAG and order[i - LAG][0] != 0:
            third[order[i - LAG]].wait_recv()
            send_fourth(*order[i - LAG])
    for key in order[len(order) - LAG:]:
        third[key].wait_recv()
        send_fourth(*key)
    for db in HOPS:
        third[0, db].wait_recv()
    for copy in fourth.values():
        copy.wait_recv()

    def where_home(side):
        slot = slot_of_side[side]
        p = slot // CAP
        dy = lax.rem(p // 4 + 4 - y, 4)
        dz = lax.rem(lax.rem(p, 4) + 4 - z, 4)
        da = jnp.where(core == 0, dy, dz)
        db = jnp.where(core == 0, dz, dy)
        return (da * 4 + db) * CAP + lax.rem(slot, CAP), offsets[aux * 16 + p]

    flat = home.reshape(16 * CAP, npno, fit)
    per = tile // npno
    lane = lax.broadcasted_iota(jnp.int32, (npno, fit), 1)
    for half in range(out_ref.shape[0] // per):
        for i in range(per):
            n = half * per + i
            at_0, off_0 = where_home(2 * n)
            at_1, off_1 = where_home(2 * n + 1)
            low, high = jnp.minimum(off_0, off_1), jnp.maximum(off_0, off_1)
            one = flat[at_0]
            outside = jnp.logical_and(lane >= low, lane < high)
            left[pl.ds(i * npno, npno), :] = jnp.where(outside, jnp.zeros_like(one), one)
            right[pl.ds(i * npno, npno), :] = flat[at_1]
        both = lax.dot_general(
            left[...], right[...], (((1,), (1,)), ((), ())), preferred_element_type=jnp.float32
        )
        for i in range(per):
            out_ref[half * per + i] = both[
                i * npno:(i + 1) * npno, i * npno:(i + 1) * npno
            ]

    for copy in raw_copies:
        copy.wait_send()
    for group in (first, second, third, fourth):
        for copy in group.values():
            copy.wait_send()


def on_device(raw_ints, fit_inverse, pair_orbs, pno_coef, pno_energy, occ_energy, fit_offset):
    region = lax.axis_index("aux")
    orb_count = lax.axis_size("orb")
    pairs, _, npno, dom = pno_coef.shape
    fit = fit_inverse.shape[1]
    side_count = 2 * pairs
    side_orbs = pair_orbs.reshape(side_count)
    sequence = jnp.arange(side_count, dtype=jnp.int32)
    same = side_orbs[:, None] == side_orbs[None, :]
    earlier = sequence[None, :] < sequence[:, None]
    slot_of_side = side_orbs * CAP + jnp.sum(jnp.where(same & earlier, 1, 0), axis=1)
    slots = jnp.arange(orb_count * CAP, dtype=jnp.int32)
    side_of_slot = jnp.sum(
        jnp.where(slots[:, None] == slot_of_side[None, :], sequence[None, :], 0), axis=1
    )
    bf16 = jnp.bfloat16
    vmem = pltpu.VMEM
    dma = pltpu.SemaphoreType.DMA
    smem_spec = pl.BlockSpec(memory_space=pltpu.SMEM)
    any_spec = pl.BlockSpec(memory_space=pl.ANY)
    coupling = pl.pallas_call(
        exchange_kernel,
        out_shape=jax.ShapeDtypeStruct((pairs, npno, npno), jnp.float32),
        in_specs=[smem_spec] * 3 + [any_spec] * 3,
        out_specs=pl.BlockSpec(memory_space=pltpu.VMEM),
        scratch_shapes=[
            vmem((side_count, npno, dom), bf16),
            vmem((fit, fit), bf16),
            vmem((fit, fit), bf16),
            vmem((fit, dom), bf16),
            vmem((dom, fit), bf16),
            vmem((4, 4, CAP, npno, dom), bf16),
            vmem((3, 4, CAP, npno, dom), bf16),
            vmem((4, 3, CAP, npno, dom), bf16),
            vmem((4, 4, CAP, npno, fit), bf16),
            vmem((3, 3, CAP, npno, fit), bf16),
            vmem((4, 4, CAP, npno, fit), bf16),
            vmem((256, fit), bf16),
            vmem((256, fit), bf16),
            dma((3,)), dma((7,)), dma((7,)),
            dma((12,)), dma((12,)), dma((12,)), dma((12,)),
            dma((12,)), dma((12,)), dma((12,)), dma((12,)),
        ],
        compiler_params=pltpu.CompilerParams(
            collective_id=0, has_side_effects=True, vmem_limit_bytes=56 * 2**20
        ),
        name="exchange",
    )(
        side_of_slot, slot_of_side, fit_offset,
        raw_ints, fit_inverse, pno_coef.reshape(side_count, npno, dom),
    )
    global_orb = region * orb_count + pair_orbs
    orbitals = jnp.arange(occ_energy.shape[0], dtype=jnp.int32)
    selector = global_orb[:, :, None] == orbitals[None, None, :]
    occupied = jnp.sum(jnp.where(selector, occ_energy[None, None, :], 0.0), axis=2)
    denominator = (
        pno_energy[:, 0, :, None]
        + pno_energy[:, 1, None, :]
        - occupied[:, 0, None, None]
        - occupied[:, 1, None, None]
    )
    amplitude = -coupling / denominator
    energy = jnp.sum(coupling * (2.0 * amplitude - jnp.swapaxes(amplitude, 1, 2)), axis=(1, 2))
    return (amplitude.reshape(pairs, npno * npno), energy)


def solution(mesh):
    return jax.shard_map(
        on_device,
        mesh=mesh,
        in_specs=(
            P(None, "orb", "aux", None),
            P(("aux", "orb"), None, None),
            P(("aux", "orb"), None),
            P(("aux", "orb"), None, None, None),
            P(("aux", "orb"), None, None),
            P(),
            P(),
        ),
        out_specs=(P(("aux", "orb"), None), P(("aux", "orb"))),
        check_vma=False,
    )
```

```python
import jax
import jax.numpy as jnp
from jax import lax
from jax.experimental import pallas as pl
from jax.experimental.pallas import tpu as pltpu
from jax.sharding import PartitionSpec as P

MESH = pl.DeviceIdType.MESH
HOPS = (1, 3, 2)
RAW_HOPS = ((0, 1), (1, 0), (3, 0), (1, 1), (3, 1), (2, 0), (2, 1))
CAP = 4
LAG = 3
EXACT = lax.Precision.HIGHEST


def exchange_kernel(
    pair_orbs, offsets, occupied, levels, raw_ref, inv_ref, coef_ref, out_ref, energy_ref,
    coef, inverse, rolled, gathered, fitted_t, away, mid, last, sides, back, home,
    left, right, gap, spread, table, lookup,
    local_sem, raw_send, raw_recv, p1_send, p1_recv, p2_send, p2_recv,
    r1_send, r1_recv, r2_send, r2_recv,
):
    aux = lax.axis_index("aux")
    orb = lax.axis_index("orb")
    x, core = aux // 2, lax.rem(aux, 2)
    y, z = orb // 4, lax.rem(orb, 4)
    fit = inverse.shape[0]
    dom = fitted_t.shape[0]
    side_count, npno, _ = coef.shape
    pairs = side_count // 2
    rows = raw_ref.shape[2]

    def turned(d_first, d_second):
        dy = jnp.where(core == 0, d_first, d_second)
        dz = jnp.where(core == 0, d_second, d_first)
        return lax.rem(y + dy, 4) * 4 + lax.rem(z + dz, 4)

    def raw_peer(dx, dc):
        return lax.rem(x + dx, 4) * 2 + lax.rem(core + dc, 2)

    load_coef = pltpu.make_async_copy(coef_ref, coef, local_sem.at[0])
    load_inverse = pltpu.make_async_copy(inv_ref.at[0], inverse, local_sem.at[1])
    load_own = pltpu.make_async_copy(
        raw_ref.at[aux, 0], gathered.at[pl.ds(aux * rows, rows)], local_sem.at[2]
    )
    load_coef.start()
    load_inverse.start()
    load_own.start()

    barrier = pltpu.get_barrier_semaphore()
    for d in HOPS:
        pl.semaphore_signal(barrier, 1, device_id=(aux, turned(d, 0)), device_id_type=MESH)
        pl.semaphore_signal(barrier, 1, device_id=(aux, turned(0, d)), device_id_type=MESH)
    for hop in RAW_HOPS:
        pl.semaphore_signal(barrier, 1, device_id=(raw_peer(*hop), orb), device_id_type=MESH)

    lane = lax.broadcasted_iota(jnp.int32, (8, 128), 1)
    slot_orb, slot_place = lane // CAP, jnp.bitwise_and(lane, CAP - 1)
    zero = jnp.zeros((8, 128), jnp.int32)
    in_slot, seen, own_orb, place = zero, zero, zero, zero
    for i in range(side_count):
        name = pair_orbs[i // 2, i % 2]
        match = slot_orb == name
        in_slot = jnp.where(jnp.logical_and(match, seen == slot_place), i, in_slot)
        seen = seen + jnp.where(match, 1, 0)
        own_orb = jnp.where(lane == i, name, own_orb)
    for i in range(side_count):
        name = pair_orbs[i // 2, i % 2]
        place = place + jnp.where(jnp.logical_and(own_orb == name, lane > i), 1, 0)
    dy = jnp.bitwise_and(own_orb // 4 + 4 - y, 3)
    dz = jnp.bitwise_and(own_orb + 4 - z, 3)
    along = jnp.where(core == 0, dy, dz)
    across = jnp.where(core == 0, dz, dy)
    home_slot = (along * 4 + across) * CAP + jnp.minimum(place, CAP - 1)
    first_row = lax.broadcasted_iota(jnp.int32, (8, 128), 0) == 0
    table[...] = jnp.where(first_row, in_slot, home_slot)
    load_table = pltpu.make_async_copy(table, lookup, local_sem.at[3])
    load_table.start()

    pl.semaphore_wait(barrier, 2 * len(HOPS) + len(RAW_HOPS))
    raw_copies = []
    for i, hop in enumerate(RAW_HOPS):
        peer = raw_peer(*hop)
        raw_copies.append(
            pltpu.make_async_remote_copy(
                src_ref=raw_ref.at[peer, 0],
                dst_ref=gathered.at[pl.ds(aux * rows, rows)],
                send_sem=raw_send.at[i],
                recv_sem=raw_recv.at[i],
                device_id=(peer, orb),
                device_id_type=MESH,
            )
        )
        raw_copies[-1].start()

    def stage(da, db):
        base = turned(da, db) * CAP
        for j in range(CAP):
            away[da, db, j] = coef[lookup[0, base + j]]

    first, second, third, fourth = {}, {}, {}, {}

    def send_first(da, db):
        k = (da - 1) * 4 + db
        first[da, db] = pltpu.make_async_remote_copy(
            src_ref=away.at[da, db], dst_ref=mid.at[da - 1, db],
            send_sem=p1_send.at[k], recv_sem=p1_recv.at[k],
            device_id=(aux, turned(da, 0)), device_id_type=MESH,
        )
        first[da, db].start()

    def send_second(da, db):
        k = da * 3 + db - 1
        source = away.at[0, db] if da == 0 else mid.at[da - 1, db]
        second[da, db] = pltpu.make_async_remote_copy(
            src_ref=source, dst_ref=last.at[da, db - 1],
            send_sem=p2_send.at[k], recv_sem=p2_recv.at[k],
            device_id=(aux, turned(0, db)), device_id_type=MESH,
        )
        second[da, db].start()

    def send_third(da, db):
        k = da * 3 + db - 1
        target = home.at[0, db] if da == 0 else back.at[da - 1, db - 1]
        third[da, db] = pltpu.make_async_remote_copy(
            src_ref=sides.at[da, db], dst_ref=target,
            send_sem=r1_send.at[k], recv_sem=r1_recv.at[k],
            device_id=(aux, turned(0, 4 - db)), device_id_type=MESH,
        )
        third[da, db].start()

    def send_fourth(da, db):
        k = (da - 1) * 4 + db
        source = sides.at[da, 0] if db == 0 else back.at[da - 1, db - 1]
        fourth[da, db] = pltpu.make_async_remote_copy(
            src_ref=source, dst_ref=home.at[da, db],
            send_sem=r2_send.at[k], recv_sem=r2_recv.at[k],
            device_id=(aux, turned(4 - da, 0)), device_id_type=MESH,
        )
        fourth[da, db].start()

    load_coef.wait()
    load_table.wait()
    for db in (1, 3, 2, 0):
        for da in HOPS:
            stage(da, db)
            send_first(da, db)
        if db != 0:
            stage(0, db)
            send_second(0, db)
    stage(0, 0)

    wide = pairs * npno
    of_lane = lax.broadcasted_iota(jnp.int32, (pairs, wide), 1) // npno
    in_pair = of_lane == lax.broadcasted_iota(jnp.int32, (pairs, wide), 0)
    repeat = jnp.where(
        lax.broadcasted_iota(jnp.int32, (npno, wide), 0)
        == jnp.bitwise_and(lax.broadcasted_iota(jnp.int32, (npno, wide), 1), npno - 1),
        1.0, 0.0,
    )
    choose = jnp.where(in_pair, 1.0, 0.0)
    pair_lane = lax.broadcasted_iota(jnp.int32, (1, wide), 1) // npno
    filled = jnp.zeros((1, wide), jnp.float32)
    for n in range(pairs):
        both_occupied = (
            occupied[aux * 16 + pair_orbs[n, 0]] + occupied[aux * 16 + pair_orbs[n, 1]]
        )
        filled = jnp.where(pair_lane == n, both_occupied, filled)
    down, along_lanes = [], []
    for k in range(2):
        level = levels[:, k, :]
        down.append(
            lax.dot_general(
                level, choose, (((0,), (0,)), ((), ())), precision=EXACT,
                preferred_element_type=jnp.float32,
            )
        )
        every = jnp.dot(level, repeat, precision=EXACT, preferred_element_type=jnp.float32)
        along_lanes.append(jnp.sum(jnp.where(in_pair, every, 0.0), axis=0, keepdims=True))
    gap[0] = down[0] + along_lanes[1] - filled
    gap[1] = down[1] + along_lanes[0] - filled

    load_inverse.wait()
    own_offset = offsets[aux * 16 + orb]
    tile = 256

    def turn(n, carry):
        start = pl.multiple_of(n * tile, tile)
        to_row = lax.broadcasted_iota(jnp.int32, (tile, fit), 0) + start
        from_row = lax.broadcasted_iota(jnp.int32, (tile, fit), 1)
        hit = jnp.bitwise_and(to_row - from_row - own_offset + 2 * fit, fit - 1) == 0
        pick = jnp.where(hit, 1.0, 0.0).astype(jnp.bfloat16)
        rolled[pl.ds(start, tile), :] = jnp.dot(
            pick, inverse[...], preferred_element_type=jnp.float32
        ).astype(jnp.bfloat16)
        return carry

    lax.fori_loop(0, fit // tile, turn, 0)

    for db in HOPS:
        for da in HOPS:
            first[da, db].wait_recv()
            send_second(da, db)
    for da in HOPS:
        first[da, 0].wait_recv()

    load_own.wait()
    for copy in raw_copies:
        copy.wait_recv()

    def fit_tile(n, carry):
        start = pl.multiple_of(n * tile, tile)
        block = jnp.dot(
            rolled[...], gathered[:, pl.ds(start, tile)], preferred_element_type=jnp.float32
        ).astype(jnp.bfloat16)
        fitted_t[pl.ds(start, tile), :] = block.T
        return carry

    lax.fori_loop(0, dom // tile, fit_tile, 0)

    def project(source, target):
        def columns(n, carry):
            start = pl.multiple_of(n * tile, tile)
            lhs = source[...].reshape(CAP * npno, dom)
            block = jnp.dot(
                lhs, fitted_t[:, pl.ds(start, tile)], preferred_element_type=jnp.float32
            ).astype(jnp.bfloat16)
            target[:, :, pl.ds(start, tile)] = block.reshape(CAP, npno, tile)
            return carry

        lax.fori_loop(0, fit // tile, columns, 0)

    for da in HOPS:
        project(mid.at[da - 1, 0], sides.at[da, 0])
        send_fourth(da, 0)
    project(away.at[0, 0], home.at[0, 0])
    order = [(0, db) for db in HOPS] + [(da, db) for db in HOPS for da in HOPS]
    for i, (da, db) in enumerate(order):
        second[da, db].wait_recv()
        project(last.at[da, db - 1], sides.at[da, db])
        send_third(da, db)
        if i >= LAG and order[i - LAG][0] != 0:
            third[order[i - LAG]].wait_recv()
            send_fourth(*order[i - LAG])
    for key in order[len(order) - LAG:]:
        third[key].wait_recv()
        send_fourth(*key)
    for db in HOPS:
        third[0, db].wait_recv()
    for copy in fourth.values():
        copy.wait_recv()

    flat = home.reshape(16 * CAP, npno, fit)
    per = tile // npno
    lanes = 128
    packed = lanes // npno
    fit_lane = lax.broadcasted_iota(jnp.int32, (npno, fit), 1)
    block_of = lax.broadcasted_iota(jnp.int32, (npno, lanes), 1) // npno
    contract = (((1,), (1,)), ((), ()))
    energies = jnp.zeros((1, lanes), jnp.float32)
    one_lane = lax.broadcasted_iota(jnp.int32, (1, lanes), 1)
    for half in range(pairs // per):
        for i in range(per):
            n = half * per + i
            off_0 = offsets[aux * 16 + pair_orbs[n, 0]]
            off_1 = offsets[aux * 16 + pair_orbs[n, 1]]
            low, high = jnp.minimum(off_0, off_1), jnp.maximum(off_0, off_1)
            one = flat[lookup[1, 2 * n]]
            outside = jnp.logical_and(fit_lane >= low, fit_lane < high)
            left[pl.ds(i * npno, npno), :] = jnp.where(outside, jnp.zeros_like(one), one)
            right[pl.ds(i * npno, npno), :] = flat[lookup[1, 2 * n + 1]]
        ahead = lax.dot_general(
            left[...], right[...], contract, preferred_element_type=jnp.float32
        )
        behind = lax.dot_general(
            right[...], left[...], contract, preferred_element_type=jnp.float32
        )
        for part in range(per // packed):
            forward = jnp.zeros((npno, lanes), jnp.float32)
            swapped = jnp.zeros((npno, lanes), jnp.float32)
            for i in range(packed):
                at = (part * packed + i) * npno
                here = block_of == i
                cut = slice(part * lanes, (part + 1) * lanes)
                forward = jnp.where(here, ahead[at:at + npno, cut], forward)
                swapped = jnp.where(here, behind[at:at + npno, cut], swapped)
            first_pair = half * per + part * packed
            span = pl.ds(first_pair * npno, lanes)
            amplitude = -forward / gap[0, :, span]
            mirrored = -swapped / gap[1, :, span]
            share = jnp.sum(
                forward * (2.0 * amplitude - mirrored), axis=0, keepdims=True
            )
            for shift in (1, 2, 4, 8, 16):
                share = share + pltpu.roll(share, lanes - shift, 1)
            for i in range(packed):
                n = first_pair + i
                energies = jnp.where(
                    one_lane == n, pltpu.roll(share, (n - i * npno) % lanes, 1), energies
                )
            spread[...] = amplitude
            strided = [spread[pl.ds(u, npno // packed, stride=packed), :] for u in range(packed)]
            for i in range(packed):
                line = jnp.zeros((npno // packed, lanes), jnp.float32)
                for u in range(packed):
                    moved = pltpu.roll(strided[u], ((u - i) * npno) % lanes, 1)
                    line = jnp.where(block_of[:npno // packed] == u, moved, line)
                n = first_pair + i
                for t in range(npno // packed):
                    out_ref[n:n + 1, t * lanes:(t + 1) * lanes] = line[t:t + 1]
    energy_ref[...] = energies

    for copy in raw_copies:
        copy.wait_send()
    for group in (first, second, third, fourth):
        for copy in group.values():
            copy.wait_send()


def on_device(raw_ints, fit_inverse, pair_orbs, pno_coef, pno_energy, occ_energy, fit_offset):
    pairs, _, npno, dom = pno_coef.shape
    fit = fit_inverse.shape[1]
    bf16 = jnp.bfloat16
    f32 = jnp.float32
    vmem = pltpu.VMEM
    dma = pltpu.SemaphoreType.DMA
    smem_spec = pl.BlockSpec(memory_space=pltpu.SMEM)
    vmem_spec = pl.BlockSpec(memory_space=pltpu.VMEM)
    any_spec = pl.BlockSpec(memory_space=pl.ANY)
    amplitude, energy = pl.pallas_call(
        exchange_kernel,
        out_shape=(
            jax.ShapeDtypeStruct((pairs, npno * npno), f32),
            jax.ShapeDtypeStruct((1, 128), f32),
        ),
        in_specs=[smem_spec] * 3 + [vmem_spec] + [any_spec] * 3,
        out_specs=(vmem_spec, vmem_spec),
        scratch_shapes=[
            vmem((2 * pairs, npno, dom), bf16),
            vmem((fit, fit), bf16),
            vmem((fit, fit), bf16),
            vmem((fit, dom), bf16),
            vmem((dom, fit), bf16),
            vmem((4, 4, CAP, npno, dom), bf16),
            vmem((3, 4, CAP, npno, dom), bf16),
            vmem((4, 3, CAP, npno, dom), bf16),
            vmem((4, 4, CAP, npno, fit), bf16),
            vmem((3, 3, CAP, npno, fit), bf16),
            vmem((4, 4, CAP, npno, fit), bf16),
            vmem((256, fit), bf16),
            vmem((256, fit), bf16),
            vmem((2, npno, pairs * npno), f32),
            vmem((npno, 128), f32),
            vmem((8, 128), jnp.int32),
            pltpu.SMEM((8, 128), jnp.int32),
            dma((4,)), dma((7,)), dma((7,)),
            dma((12,)), dma((12,)), dma((12,)), dma((12,)),
            dma((12,)), dma((12,)), dma((12,)), dma((12,)),
        ],
        compiler_params=pltpu.CompilerParams(
            collective_id=0, has_side_effects=True, vmem_limit_bytes=56 * 2**20
        ),
        name="exchange",
    )(
        pair_orbs, fit_offset, occ_energy, pno_energy,
        raw_ints, fit_inverse, pno_coef.reshape(2 * pairs, npno, dom),
    )
    return amplitude, energy[0, :pairs]


def solution(mesh):
    return jax.shard_map(
        on_device,
        mesh=mesh,
        in_specs=(
            P(None, "orb", "aux", None),
            P(("aux", "orb"), None, None),
            P(("aux", "orb"), None),
            P(("aux", "orb"), None, None, None),
            P(("aux", "orb"), None, None),
            P(),
            P(),
        ),
        out_specs=(P(("aux", "orb"), None), P(("aux", "orb"))),
        check_vma=False,
    )
```

```python
import jax
import jax.numpy as jnp
from jax import lax
from jax.experimental import pallas as pl
from jax.experimental.pallas import tpu as pltpu
from jax.sharding import PartitionSpec as P

MESH = pl.DeviceIdType.MESH
HOPS = (1, 3, 2)
RAW_HOPS = ((0, 1), (1, 0), (3, 0), (1, 1), (3, 1), (2, 0), (2, 1))
CAP = 4
ROW = 12
SENDS = {8: 1, 11: 3}
EXACT = lax.Precision.HIGHEST


def exchange_kernel(
    pair_orbs, offsets, occupied, levels, raw_ref, inv_ref, coef_ref,
    out_ref, energy_ref, crowded_ref,
    coef, inverse, rolled, gathered, fitted_t, packed_out, mid_1, mid_2, mid_3, away, last,
    sides, back_1, back_2, back_3, packed_back, home,
    left, right, gap, spread, table, note, notes, flags_out, flags_across, flags_aux,
    lookup, notices,
    local_sem, raw_send, raw_recv, p1_send, p1_recv, p2_send, p2_recv,
    r1_send, r1_recv, r2_send, r2_recv, note_send, note_recv, note_sem,
    across_send, across_recv, aux_send, aux_recv,
):
    mid = {1: mid_1, 2: mid_2, 3: mid_3}
    back = {1: back_1, 2: back_2, 3: back_3}
    aux = lax.axis_index("aux")
    orb = lax.axis_index("orb")
    x, core = aux // 2, lax.rem(aux, 2)
    y, z = orb // 4, lax.rem(orb, 4)
    fit = inverse.shape[0]
    dom = fitted_t.shape[0]
    side_count, npno, _ = coef.shape
    pairs = side_count // 2
    rows = raw_ref.shape[2]

    def turned(d_first, d_second):
        dy = jnp.where(core == 0, d_first, d_second)
        dz = jnp.where(core == 0, d_second, d_first)
        return lax.rem(y + dy, 4) * 4 + lax.rem(z + dz, 4)

    def raw_peer(dx, dc):
        return lax.rem(x + dx, 4) * 2 + lax.rem(core + dc, 2)

    load_coef = pltpu.make_async_copy(coef_ref, coef, local_sem.at[0])
    load_inverse = pltpu.make_async_copy(inv_ref.at[0], inverse, local_sem.at[1])
    load_own = pltpu.make_async_copy(
        raw_ref.at[aux, 0], gathered.at[pl.ds(aux * rows, rows)], local_sem.at[2]
    )
    load_coef.start()
    load_inverse.start()
    load_own.start()

    barrier = pltpu.get_barrier_semaphore()
    for d in HOPS:
        pl.semaphore_signal(barrier, 1, device_id=(aux, turned(d, 0)), device_id_type=MESH)
        pl.semaphore_signal(barrier, 1, device_id=(aux, turned(0, d)), device_id_type=MESH)
    for hop in RAW_HOPS:
        pl.semaphore_signal(barrier, 1, device_id=(raw_peer(*hop), orb), device_id_type=MESH)

    own_along = jnp.where(core == 0, y, z)
    own_across = jnp.where(core == 0, z, y)

    def row_of(p):
        return jnp.where(core == 0, p // 4, jnp.bitwise_and(p, 3))

    def place_in_row(p):
        return jnp.where(core == 0, jnp.bitwise_and(p, 3), p // 4)

    lane = lax.broadcasted_iota(jnp.int32, (8, 128), 1)
    slot_orb, slot_place = lane // CAP, jnp.bitwise_and(lane, CAP - 1)
    slot_row = row_of(slot_orb)
    list_row, list_place = lane // 16, jnp.bitwise_and(lane, 15)
    zero = jnp.zeros((8, 128), jnp.int32)
    in_slot, in_list, list_orb, slot_list = zero, zero, zero, zero
    seen, seen_row, seen_list, own_orb = zero, zero, zero, zero
    for i in range(side_count):
        name = pair_orbs[i % 2, i // 2]
        row = row_of(name)
        match = slot_orb == name
        hit = jnp.logical_and(match, seen == slot_place)
        in_slot = jnp.where(hit, i, in_slot)
        slot_list = jnp.where(hit, seen_row, slot_list)
        seen = seen + jnp.where(match, 1, 0)
        seen_row = seen_row + jnp.where(slot_row == row, 1, 0)
        match = list_row == row
        hit = jnp.logical_and(match, seen_list == list_place)
        in_list = jnp.where(hit, i, in_list)
        list_orb = jnp.where(hit, name, list_orb)
        seen_list = seen_list + jnp.where(match, 1, 0)
        own_orb = jnp.where(lane == i, name, own_orb)
    own_row = row_of(own_orb)
    side_place, side_list, list_spot = zero, zero, zero
    for i in range(side_count):
        name = pair_orbs[i % 2, i // 2]
        after = lane > i
        side_place = side_place + jnp.where(jnp.logical_and(own_orb == name, after), 1, 0)
        side_list = side_list + jnp.where(
            jnp.logical_and(own_row == row_of(name), after), 1, 0
        )
        list_spot = list_spot + jnp.where(
            jnp.logical_and(list_orb == name, in_list > i), 1, 0
        )
    along = jnp.bitwise_and(own_row + 4 - own_along, 3)
    across = jnp.bitwise_and(place_in_row(own_orb) + 4 - own_across, 3)
    home_slot = jnp.where(
        along == 0,
        across * CAP + jnp.minimum(side_place, CAP - 1),
        4 * CAP + (along - 1) * ROW + jnp.minimum(side_list, ROW - 1),
    )
    list_slot = (
        jnp.bitwise_and(place_in_row(list_orb) + 4 - own_across, 3) * CAP
        + jnp.minimum(list_spot, CAP - 1)
    )
    crowded = jnp.max(jnp.where(jnp.logical_and(list_row < 4, seen_list > ROW), 1, 0))
    row_at = lax.broadcasted_iota(jnp.int32, (8, 128), 0)
    table[...] = jnp.where(row_at == 0, in_slot, jnp.where(row_at == 1, home_slot, in_list))
    note[...] = jnp.where(
        row_at == 0,
        jnp.minimum(slot_list, ROW - 1),
        jnp.where(row_at == 1, list_slot, crowded),
    )
    load_table = pltpu.make_async_copy(table, lookup, local_sem.at[3])
    load_table.start()

    pl.semaphore_wait(barrier, 2 * len(HOPS) + len(RAW_HOPS))
    raw_copies = []
    for i, hop in enumerate(RAW_HOPS):
        peer = raw_peer(*hop)
        raw_copies.append(
            pltpu.make_async_remote_copy(
                src_ref=raw_ref.at[peer, 0],
                dst_ref=gathered.at[pl.ds(aux * rows, rows)],
                send_sem=raw_send.at[i],
                recv_sem=raw_recv.at[i],
                device_id=(peer, orb),
                device_id_type=MESH,
            )
        )
        raw_copies[-1].start()

    told, first, second, third, fourth = {}, {}, {}, {}, {}

    def tell(da):
        told[da] = pltpu.make_async_remote_copy(
            src_ref=note, dst_ref=notes.at[da - 1],
            send_sem=note_send.at[da - 1], recv_sem=note_recv.at[da - 1],
            device_id=(aux, turned(da, 0)), device_id_type=MESH,
        )
        told[da].start()

    def send_first(da):
        first[da] = pltpu.make_async_remote_copy(
            src_ref=packed_out.at[da - 1], dst_ref=mid[da],
            send_sem=p1_send.at[da - 1], recv_sem=p1_recv.at[da - 1],
            device_id=(aux, turned(da, 0)), device_id_type=MESH,
        )
        first[da].start()

    def send_second(da, db):
        k = da * 3 + db - 1
        second[da, db] = pltpu.make_async_remote_copy(
            src_ref=away.at[da, db], dst_ref=last.at[da, db - 1],
            send_sem=p2_send.at[k], recv_sem=p2_recv.at[k],
            device_id=(aux, turned(0, db)), device_id_type=MESH,
        )
        second[da, db].start()

    def send_third(da, db):
        k = da * 3 + db - 1
        spots = pl.ds(db * CAP, CAP)
        third[da, db] = pltpu.make_async_remote_copy(
            src_ref=sides.at[da, db - 1],
            dst_ref=home.at[spots] if da == 0 else back[da].at[spots],
            send_sem=r1_send.at[k], recv_sem=r1_recv.at[k],
            device_id=(aux, turned(0, 4 - db)), device_id_type=MESH,
        )
        third[da, db].start()

    def send_fourth(da):
        for db in HOPS:
            third[da, db].wait_recv()
        at = (own_along * 16)
        for q in range(ROW):
            packed_back[da - 1, q] = back[da][notices[da - 1, 1, at + q]]
        fourth[da] = pltpu.make_async_remote_copy(
            src_ref=packed_back.at[da - 1],
            dst_ref=home.at[pl.ds(4 * CAP + (da - 1) * ROW, ROW)],
            send_sem=r2_send.at[da - 1], recv_sem=r2_recv.at[da - 1],
            device_id=(aux, turned(4 - da, 0)), device_id_type=MESH,
        )
        fourth[da].start()

    for da in HOPS:
        tell(da)
    load_coef.wait()
    load_table.wait()
    for da in HOPS:
        to_row = jnp.bitwise_and(own_along + da, 3) * 16
        for q in range(ROW):
            packed_out[da - 1, q] = coef[lookup[2, to_row + q]]
        send_first(da)
    for db in (1, 3, 2, 0):
        base = turned(0, db) * CAP
        for j in range(CAP):
            away[0, db, j] = coef[lookup[0, base + j]]
        if db != 0:
            send_second(0, db)

    wide = pairs * npno
    of_lane = lax.broadcasted_iota(jnp.int32, (pairs, wide), 1) // npno
    in_pair = of_lane == lax.broadcasted_iota(jnp.int32, (pairs, wide), 0)
    repeat = jnp.where(
        lax.broadcasted_iota(jnp.int32, (npno, wide), 0)
        == jnp.bitwise_and(lax.broadcasted_iota(jnp.int32, (npno, wide), 1), npno - 1),
        1.0, 0.0,
    )
    choose = jnp.where(in_pair, 1.0, 0.0)
    pair_lane = lax.broadcasted_iota(jnp.int32, (1, wide), 1) // npno
    filled = jnp.zeros((1, wide), jnp.float32)
    for n in range(pairs):
        both_occupied = (
            occupied[aux * 16 + pair_orbs[0, n]] + occupied[aux * 16 + pair_orbs[1, n]]
        )
        filled = jnp.where(pair_lane == n, both_occupied, filled)
    down, along_lanes = [], []
    for k in range(2):
        level = levels[:, k, :]
        down.append(
            lax.dot_general(
                level, choose, (((0,), (0,)), ((), ())), precision=EXACT,
                preferred_element_type=jnp.float32,
            )
        )
        every = jnp.dot(level, repeat, precision=EXACT, preferred_element_type=jnp.float32)
        along_lanes.append(jnp.sum(jnp.where(in_pair, every, 0.0), axis=0, keepdims=True))
    gap[0] = down[0] + along_lanes[1] - filled
    gap[1] = down[1] + along_lanes[0] - filled

    load_inverse.wait()
    own_offset = offsets[aux * 16 + orb]
    tile = 256

    def turn(n, carry):
        start = pl.multiple_of(n * tile, tile)
        to_row = lax.broadcasted_iota(jnp.int32, (tile, fit), 0) + start
        from_row = lax.broadcasted_iota(jnp.int32, (tile, fit), 1)
        hit = jnp.bitwise_and(to_row - from_row - own_offset + 2 * fit, fit - 1) == 0
        pick = jnp.where(hit, 1.0, 0.0).astype(jnp.bfloat16)
        rolled[pl.ds(start, tile), :] = jnp.dot(
            pick, inverse[...], preferred_element_type=jnp.float32
        ).astype(jnp.bfloat16)
        return carry

    lax.fori_loop(0, fit // tile, turn, 0)

    unread = []
    for da in HOPS:
        told[da].wait_recv()
        unread.append(
            pltpu.make_async_copy(notes.at[da - 1], notices.at[da - 1], note_sem.at[da - 1])
        )
        unread[-1].start()
    flags_out[0] = jnp.maximum(
        jnp.maximum(notes[0], notes[1]), jnp.maximum(notes[2], note[...])
    )
    flag_copies = []
    for db in HOPS:
        flag_copies.append(
            pltpu.make_async_remote_copy(
                src_ref=flags_out.at[0], dst_ref=flags_across.at[db - 1],
                send_sem=across_send.at[db - 1], recv_sem=across_recv.at[db - 1],
                device_id=(aux, turned(0, db)), device_id_type=MESH,
            )
        )
        flag_copies[-1].start()
    for copy in unread:
        copy.wait()

    for da in HOPS:
        first[da].wait_recv()
        for db in (1, 3, 2, 0):
            base = turned(0, db) * CAP
            for j in range(CAP):
                away[da, db, j] = mid[da][notices[da - 1, 0, base + j]]
            if db != 0:
                send_second(da, db)

    for copy in flag_copies:
        copy.wait()
    flags_out[1] = jnp.maximum(
        jnp.maximum(flags_across[0], flags_across[1]),
        jnp.maximum(flags_across[2], flags_out[0]),
    )
    last_flags = []
    for i, hop in enumerate(RAW_HOPS):
        last_flags.append(
            pltpu.make_async_remote_copy(
                src_ref=flags_out.at[1], dst_ref=flags_aux.at[i],
                send_sem=aux_send.at[i], recv_sem=aux_recv.at[i],
                device_id=(raw_peer(*hop), orb), device_id_type=MESH,
            )
        )
        last_flags[-1].start()

    load_own.wait()
    for copy in raw_copies:
        copy.wait_recv()

    def fit_tile(n, carry):
        start = pl.multiple_of(n * tile, tile)
        block = jnp.dot(
            rolled[...], gathered[:, pl.ds(start, tile)], preferred_element_type=jnp.float32
        ).astype(jnp.bfloat16)
        fitted_t[pl.ds(start, tile), :] = block.T
        return carry

    lax.fori_loop(0, dom // tile, fit_tile, 0)

    def project(source, target):
        def columns(n, carry):
            start = pl.multiple_of(n * tile, tile)
            lhs = source[...].reshape(CAP * npno, dom)
            block = jnp.dot(
                lhs, fitted_t[:, pl.ds(start, tile)], preferred_element_type=jnp.float32
            ).astype(jnp.bfloat16)
            target[:, :, pl.ds(start, tile)] = block.reshape(CAP, npno, tile)
            return carry

        lax.fori_loop(0, fit // tile, columns, 0)

    for da in HOPS:
        project(away.at[da, 0], back[da].at[pl.ds(0, CAP)])
    project(away.at[0, 0], home.at[pl.ds(0, CAP)])
    order = [(da, db) for da in (0, 1, 3, 2) for db in HOPS]
    for i, (da, db) in enumerate(order):
        second[da, db].wait_recv()
        project(last.at[da, db - 1], sides.at[da, db - 1])
        send_third(da, db)
        if i in SENDS:
            send_fourth(SENDS[i])
    send_fourth(2)
    for db in HOPS:
        third[0, db].wait_recv()
    for da in HOPS:
        fourth[da].wait_recv()

    per = tile // npno
    lanes = 128
    packed = lanes // npno
    fit_lane = lax.broadcasted_iota(jnp.int32, (npno, fit), 1)
    block_of = lax.broadcasted_iota(jnp.int32, (npno, lanes), 1) // npno
    contract = (((1,), (1,)), ((), ()))
    energies = jnp.zeros((1, lanes), jnp.float32)
    one_lane = lax.broadcasted_iota(jnp.int32, (1, lanes), 1)
    for half in range(pairs // per):
        for i in range(per):
            n = half * per + i
            off_0 = offsets[aux * 16 + pair_orbs[0, n]]
            off_1 = offsets[aux * 16 + pair_orbs[1, n]]
            low, high = jnp.minimum(off_0, off_1), jnp.maximum(off_0, off_1)
            one = home[lookup[1, 2 * n]]
            outside = jnp.logical_and(fit_lane >= low, fit_lane < high)
            left[pl.ds(i * npno, npno), :] = jnp.where(outside, jnp.zeros_like(one), one)
            right[pl.ds(i * npno, npno), :] = home[lookup[1, 2 * n + 1]]
        ahead = lax.dot_general(
            left[...], right[...], contract, preferred_element_type=jnp.float32
        )
        behind = lax.dot_general(
            right[...], left[...], contract, preferred_element_type=jnp.float32
        )
        for part in range(per // packed):
            forward = jnp.zeros((npno, lanes), jnp.float32)
            swapped = jnp.zeros((npno, lanes), jnp.float32)
            for i in range(packed):
                at = (part * packed + i) * npno
                here = block_of == i
                cut = slice(part * lanes, (part + 1) * lanes)
                forward = jnp.where(here, ahead[at:at + npno, cut], forward)
                swapped = jnp.where(here, behind[at:at + npno, cut], swapped)
            first_pair = half * per + part * packed
            span = pl.ds(first_pair * npno, lanes)
            amplitude = -forward / gap[0, :, span]
            mirrored = -swapped / gap[1, :, span]
            share = jnp.sum(
                forward * (2.0 * amplitude - mirrored), axis=0, keepdims=True
            )
            for shift in (1, 2, 4, 8, 16):
                share = share + pltpu.roll(share, lanes - shift, 1)
            for i in range(packed):
                n = first_pair + i
                energies = jnp.where(
                    one_lane == n, pltpu.roll(share, (n - i * npno) % lanes, 1), energies
                )
            spread[...] = amplitude
            strided = [spread[pl.ds(u, npno // packed, stride=packed), :] for u in range(packed)]
            for i in range(packed):
                line = jnp.zeros((npno // packed, lanes), jnp.float32)
                for u in range(packed):
                    moved = pltpu.roll(strided[u], ((u - i) * npno) % lanes, 1)
                    line = jnp.where(block_of[:npno // packed] == u, moved, line)
                n = first_pair + i
                for t in range(npno // packed):
                    out_ref[n:n + 1, t * lanes:(t + 1) * lanes] = line[t:t + 1]
    energy_ref[...] = energies
    every_flag = flags_out[1]
    for i, copy in enumerate(last_flags):
        copy.wait()
        every_flag = jnp.maximum(every_flag, flags_aux[i])
    crowded_ref[...] = every_flag

    for copy in raw_copies:
        copy.wait_send()
    for group in (told, first, second, third, fourth):
        for copy in group.values():
            copy.wait_send()


def align_rows(shifted_in, begin_at):
    return lax.dynamic_slice_in_dim(shifted_in, begin_at, shifted_in.shape[1] * 2 // 3, 1)


def spread_out(raw_ints, fit_inverse, pair_orbs, pno_coef, pno_energy, occ_energy, fit_offset):
    orb_count = lax.axis_size("orb")
    region = lax.axis_index("aux")
    inverse = fit_inverse[0]
    gathered = lax.all_to_all(raw_ints, "aux", split_axis=0, concat_axis=2, tiled=True)
    fitted = jnp.dot(inverse, gathered[0, 0], preferred_element_type=jnp.float32).astype(
        jnp.bfloat16
    )
    fit_rows = fitted.shape[0]
    pair_count = pair_orbs.shape[0]
    pno_count = pno_coef.shape[2]
    dom_count = pno_coef.shape[3]
    side_count = 2 * pair_count
    capacity = max(2, 4 * pair_count // orb_count)
    slot_count = orb_count * capacity
    side_orbs = pair_orbs.reshape(side_count)
    matches = side_orbs[:, None] == side_orbs[None, :]
    sequence = jnp.arange(side_count, dtype=jnp.int32)
    earlier = sequence[None, :] < sequence[:, None]
    position = jnp.sum(jnp.where(matches & earlier, 1, 0), axis=1)
    slot_index = side_orbs * capacity + position
    placing = jnp.where(
        slot_index[None, :] == jnp.arange(slot_count, dtype=jnp.int32)[:, None], 1.0, 0.0
    ).astype(jnp.bfloat16)
    outgoing = jnp.dot(
        placing,
        pno_coef.reshape(side_count, pno_count * dom_count),
        preferred_element_type=jnp.float32,
    ).astype(jnp.bfloat16)
    outgoing = outgoing.reshape(orb_count, capacity, pno_count, dom_count)
    projected = jnp.einsum(
        "scpd,fd->scpf",
        lax.all_to_all(outgoing, "orb", split_axis=0, concat_axis=0, tiled=True),
        fitted,
        preferred_element_type=jnp.float32,
    ).astype(jnp.bfloat16)
    returned = lax.all_to_all(projected, "orb", split_axis=0, concat_axis=0, tiled=True)
    side_blocks = jnp.dot(
        placing.T,
        returned.reshape(slot_count, pno_count * fit_rows),
        preferred_element_type=jnp.float32,
    ).astype(jnp.bfloat16)
    side_blocks = side_blocks.reshape(pair_count, 2, pno_count, fit_rows)
    orb_total = occ_energy.shape[0]
    global_orb = region * orb_count + pair_orbs
    selector = global_orb[:, :, None] == jnp.arange(orb_total, dtype=jnp.int32)[None, None, :]
    offsets = jnp.sum(jnp.where(selector, fit_offset[None, None, :], 0), axis=2)
    occupied = jnp.sum(jnp.where(selector, occ_energy[None, None, :], 0.0), axis=2)
    margin = fit_rows // 4
    shift_rows = offsets[:, 0] - offsets[:, 1]
    padded = jnp.pad(side_blocks[:, 1], ((0, 0), (0, 0), (margin, margin)))
    aligned = jax.vmap(align_rows)(padded, margin + shift_rows)
    coupling = jnp.einsum(
        "npr,nqr->npq", side_blocks[:, 0], aligned, preferred_element_type=jnp.float32
    )
    denominator = (
        pno_energy[:, 0, :, None]
        + pno_energy[:, 1, None, :]
        - occupied[:, 0, None, None]
        - occupied[:, 1, None, None]
    )
    amplitude = -coupling / denominator
    energy = jnp.sum(coupling * (2.0 * amplitude - jnp.swapaxes(amplitude, 1, 2)), axis=(1, 2))
    return (amplitude.reshape(pair_count, pno_count * pno_count), energy)


def on_device(raw_ints, fit_inverse, pair_orbs, pno_coef, pno_energy, occ_energy, fit_offset):
    pairs, _, npno, dom = pno_coef.shape
    fit = fit_inverse.shape[1]
    bf16 = jnp.bfloat16
    f32 = jnp.float32
    i32 = jnp.int32
    vmem = pltpu.VMEM
    dma = pltpu.SemaphoreType.DMA
    smem_spec = pl.BlockSpec(memory_space=pltpu.SMEM)
    vmem_spec = pl.BlockSpec(memory_space=pltpu.VMEM)
    any_spec = pl.BlockSpec(memory_space=pl.ANY)
    amplitude, energy, crowded = pl.pallas_call(
        exchange_kernel,
        out_shape=(
            jax.ShapeDtypeStruct((pairs, npno * npno), f32),
            jax.ShapeDtypeStruct((1, 128), f32),
            jax.ShapeDtypeStruct((8, 128), i32),
        ),
        in_specs=[smem_spec] * 3 + [vmem_spec] + [any_spec] * 3,
        out_specs=(vmem_spec, vmem_spec, vmem_spec),
        scratch_shapes=[
            vmem((2 * pairs, npno, dom), bf16),
            vmem((fit, fit), bf16),
            vmem((fit, fit), bf16),
            vmem((fit, dom), bf16),
            vmem((dom, fit), bf16),
            vmem((3, ROW, npno, dom), bf16),
            vmem((ROW, npno, dom), bf16),
            vmem((ROW, npno, dom), bf16),
            vmem((ROW, npno, dom), bf16),
            vmem((4, 4, CAP, npno, dom), bf16),
            vmem((4, 3, CAP, npno, dom), bf16),
            vmem((4, 3, CAP, npno, fit), bf16),
            vmem((4 * CAP, npno, fit), bf16),
            vmem((4 * CAP, npno, fit), bf16),
            vmem((4 * CAP, npno, fit), bf16),
            vmem((3, ROW, npno, fit), bf16),
            vmem((4 * CAP + 3 * ROW, npno, fit), bf16),
            vmem((256, fit), bf16),
            vmem((256, fit), bf16),
            vmem((2, npno, pairs * npno), f32),
            vmem((npno, 128), f32),
            vmem((8, 128), i32),
            vmem((8, 128), i32),
            vmem((3, 8, 128), i32),
            vmem((2, 8, 128), i32),
            vmem((3, 8, 128), i32),
            vmem((7, 8, 128), i32),
            pltpu.SMEM((8, 128), i32),
            pltpu.SMEM((3, 8, 128), i32),
            dma((4,)), dma((7,)), dma((7,)),
            dma((3,)), dma((3,)), dma((12,)), dma((12,)),
            dma((12,)), dma((12,)), dma((3,)), dma((3,)),
            dma((3,)), dma((3,)), dma((3,)),
            dma((3,)), dma((3,)), dma((7,)), dma((7,)),
        ],
        compiler_params=pltpu.CompilerParams(
            collective_id=0, has_side_effects=True, vmem_limit_bytes=58 * 2**20
        ),
        name="exchange",
    )(
        pair_orbs.T, fit_offset, occ_energy, pno_energy,
        raw_ints, fit_inverse, pno_coef.reshape(2 * pairs, npno, dom),
    )
    return lax.cond(
        crowded[2, 0] > 0,
        lambda: spread_out(
            raw_ints, fit_inverse, pair_orbs, pno_coef, pno_energy, occ_energy, fit_offset
        ),
        lambda: (amplitude, energy[0, :pairs]),
    )


def solution(mesh):
    return jax.shard_map(
        on_device,
        mesh=mesh,
        in_specs=(
            P(None, "orb", "aux", None),
            P(("aux", "orb"), None, None),
            P(("aux", "orb"), None),
            P(("aux", "orb"), None, None, None),
            P(("aux", "orb"), None, None),
            P(),
            P(),
        ),
        out_specs=(P(("aux", "orb"), None), P(("aux", "orb"))),
        check_vma=False,
    )
```

```python
import jax
import jax.numpy as jnp
from jax import lax
from jax.experimental import pallas as pl
from jax.experimental.pallas import tpu as pltpu
from jax.sharding import PartitionSpec as P

MESH = pl.DeviceIdType.MESH
HOPS = (1, 3, 2)
RAW_HOPS = ((0, 1), (1, 0), (3, 0), (1, 1), (3, 1), (2, 0), (2, 1))
CAP = 4
ROW = 11
EXACT = lax.Precision.HIGHEST


def exchange_kernel(
    pair_orbs, offsets, occupied, levels, raw_ref, inv_ref, coef_ref,
    out_ref, energy_ref, crowded_ref,
    coef, inverse, rolled, gathered, fitted_t, packed_out, mid_1, mid_2, mid_3, away, last,
    sides, back_1, back_2, back_3, packed_back, home,
    left, right, gap, spread, table, note, notes, flags_out, flags_across, flags_aux,
    lookup, notices,
    local_sem, raw_send, raw_recv, p1_send, p1_recv, p2_send, p2_recv,
    r1_send, r1_recv, r2_send, r2_recv, note_send, note_recv, note_sem,
    across_send, across_recv, aux_send, aux_recv,
):
    mid = {1: mid_1, 2: mid_2, 3: mid_3}
    back = {1: back_1, 2: back_2, 3: back_3}
    aux = lax.axis_index("aux")
    orb = lax.axis_index("orb")
    x, core = aux // 2, lax.rem(aux, 2)
    y, z = orb // 4, lax.rem(orb, 4)
    fit = inverse.shape[0]
    dom = fitted_t.shape[0]
    side_count, npno, _ = coef.shape
    pairs = side_count // 2
    rows = raw_ref.shape[2]

    def turned(d_first, d_second):
        dy = jnp.where(core == 0, d_first, d_second)
        dz = jnp.where(core == 0, d_second, d_first)
        return lax.rem(y + dy, 4) * 4 + lax.rem(z + dz, 4)

    def raw_peer(dx, dc):
        return lax.rem(x + dx, 4) * 2 + lax.rem(core + dc, 2)

    load_coef = pltpu.make_async_copy(coef_ref, coef, local_sem.at[0])
    load_inverse = pltpu.make_async_copy(inv_ref.at[0], inverse, local_sem.at[1])
    load_own = pltpu.make_async_copy(
        raw_ref.at[aux, 0], gathered.at[pl.ds(aux * rows, rows)], local_sem.at[2]
    )
    load_coef.start()
    load_inverse.start()
    load_own.start()

    barrier = pltpu.get_barrier_semaphore()
    for d in HOPS:
        pl.semaphore_signal(barrier, 1, device_id=(aux, turned(d, 0)), device_id_type=MESH)
        pl.semaphore_signal(barrier, 1, device_id=(aux, turned(0, d)), device_id_type=MESH)
    for hop in RAW_HOPS:
        pl.semaphore_signal(barrier, 1, device_id=(raw_peer(*hop), orb), device_id_type=MESH)

    own_along = jnp.where(core == 0, y, z)
    own_across = jnp.where(core == 0, z, y)

    def row_of(p):
        return jnp.where(core == 0, p // 4, jnp.bitwise_and(p, 3))

    def place_in_row(p):
        return jnp.where(core == 0, jnp.bitwise_and(p, 3), p // 4)

    lane = lax.broadcasted_iota(jnp.int32, (8, 128), 1)
    slot_orb, slot_place = lane // CAP, jnp.bitwise_and(lane, CAP - 1)
    slot_row = row_of(slot_orb)
    list_row, list_place = lane // 16, jnp.bitwise_and(lane, 15)
    zero = jnp.zeros((8, 128), jnp.int32)
    in_slot, in_list, list_orb, slot_list = zero, zero, zero, zero
    seen, seen_row, seen_list, own_orb = zero, zero, zero, zero
    for i in range(side_count):
        name = pair_orbs[i % 2, i // 2]
        row = row_of(name)
        match = slot_orb == name
        hit = jnp.logical_and(match, seen == slot_place)
        in_slot = jnp.where(hit, i, in_slot)
        slot_list = jnp.where(hit, seen_row, slot_list)
        seen = seen + jnp.where(match, 1, 0)
        seen_row = seen_row + jnp.where(slot_row == row, 1, 0)
        match = list_row == row
        hit = jnp.logical_and(match, seen_list == list_place)
        in_list = jnp.where(hit, i, in_list)
        list_orb = jnp.where(hit, name, list_orb)
        seen_list = seen_list + jnp.where(match, 1, 0)
        own_orb = jnp.where(lane == i, name, own_orb)
    own_row = row_of(own_orb)
    side_place, side_list, list_spot = zero, zero, zero
    for i in range(side_count):
        name = pair_orbs[i % 2, i // 2]
        after = lane > i
        side_place = side_place + jnp.where(jnp.logical_and(own_orb == name, after), 1, 0)
        side_list = side_list + jnp.where(
            jnp.logical_and(own_row == row_of(name), after), 1, 0
        )
        list_spot = list_spot + jnp.where(
            jnp.logical_and(list_orb == name, in_list > i), 1, 0
        )
    along = jnp.bitwise_and(own_row + 4 - own_along, 3)
    across = jnp.bitwise_and(place_in_row(own_orb) + 4 - own_across, 3)
    home_slot = jnp.where(
        along == 0,
        across * CAP + jnp.minimum(side_place, CAP - 1),
        4 * CAP + (along - 1) * ROW + jnp.minimum(side_list, ROW - 1),
    )
    list_slot = (
        jnp.bitwise_and(place_in_row(list_orb) + 4 - own_across, 3) * CAP
        + jnp.minimum(list_spot, CAP - 1)
    )
    crowded = jnp.max(jnp.where(jnp.logical_and(list_row < 4, seen_list > ROW), 1, 0))
    row_at = lax.broadcasted_iota(jnp.int32, (8, 128), 0)
    table[...] = jnp.where(row_at == 0, in_slot, jnp.where(row_at == 1, home_slot, in_list))
    note[...] = jnp.where(
        row_at == 0,
        jnp.minimum(slot_list, ROW - 1),
        jnp.where(row_at == 1, list_slot, crowded),
    )
    load_table = pltpu.make_async_copy(table, lookup, local_sem.at[3])
    load_table.start()

    pl.semaphore_wait(barrier, 2 * len(HOPS) + len(RAW_HOPS))
    raw_copies = []
    for i, hop in enumerate(RAW_HOPS):
        peer = raw_peer(*hop)
        raw_copies.append(
            pltpu.make_async_remote_copy(
                src_ref=raw_ref.at[peer, 0],
                dst_ref=gathered.at[pl.ds(aux * rows, rows)],
                send_sem=raw_send.at[i],
                recv_sem=raw_recv.at[i],
                device_id=(peer, orb),
                device_id_type=MESH,
            )
        )
        raw_copies[-1].start()

    told, first, second, third, fourth = {}, {}, {}, {}, {}

    def tell(da):
        told[da] = pltpu.make_async_remote_copy(
            src_ref=note, dst_ref=notes.at[da - 1],
            send_sem=note_send.at[da - 1], recv_sem=note_recv.at[da - 1],
            device_id=(aux, turned(da, 0)), device_id_type=MESH,
        )
        told[da].start()

    def send_first(da):
        first[da] = pltpu.make_async_remote_copy(
            src_ref=packed_out.at[da - 1], dst_ref=mid[da],
            send_sem=p1_send.at[da - 1], recv_sem=p1_recv.at[da - 1],
            device_id=(aux, turned(da, 0)), device_id_type=MESH,
        )
        first[da].start()

    def send_second(da, db):
        k = da * 3 + db - 1
        second[da, db] = pltpu.make_async_remote_copy(
            src_ref=away.at[da, db], dst_ref=last.at[da, db - 1],
            send_sem=p2_send.at[k], recv_sem=p2_recv.at[k],
            device_id=(aux, turned(0, db)), device_id_type=MESH,
        )
        second[da, db].start()

    def send_third(da, db):
        k = da * 3 + db - 1
        spots = pl.ds(db * CAP, CAP)
        third[da, db] = pltpu.make_async_remote_copy(
            src_ref=sides.at[da, db - 1],
            dst_ref=home.at[spots] if da == 0 else back[da].at[spots],
            send_sem=r1_send.at[k], recv_sem=r1_recv.at[k],
            device_id=(aux, turned(0, 4 - db)), device_id_type=MESH,
        )
        third[da, db].start()

    def send_fourth(da):
        for db in HOPS:
            third[da, db].wait_recv()
        at = (own_along * 16)
        for q in range(ROW):
            packed_back[da - 1, q] = back[da][notices[da - 1, 1, at + q]]
        fourth[da] = pltpu.make_async_remote_copy(
            src_ref=packed_back.at[da - 1],
            dst_ref=home.at[pl.ds(4 * CAP + (da - 1) * ROW, ROW)],
            send_sem=r2_send.at[da - 1], recv_sem=r2_recv.at[da - 1],
            device_id=(aux, turned(4 - da, 0)), device_id_type=MESH,
        )
        fourth[da].start()

    for da in HOPS:
        tell(da)
    load_coef.wait()
    load_table.wait()
    for da in (2, 1, 3):
        to_row = jnp.bitwise_and(own_along + da, 3) * 16
        for q in range(ROW):
            packed_out[da - 1, q] = coef[lookup[2, to_row + q]]
        send_first(da)
    for db in (1, 3, 2, 0):
        base = turned(0, db) * CAP
        for j in range(CAP):
            away[0, db, j] = coef[lookup[0, base + j]]
        if db != 0:
            send_second(0, db)

    wide = pairs * npno
    of_lane = lax.broadcasted_iota(jnp.int32, (pairs, wide), 1) // npno
    in_pair = of_lane == lax.broadcasted_iota(jnp.int32, (pairs, wide), 0)
    repeat = jnp.where(
        lax.broadcasted_iota(jnp.int32, (npno, wide), 0)
        == jnp.bitwise_and(lax.broadcasted_iota(jnp.int32, (npno, wide), 1), npno - 1),
        1.0, 0.0,
    )
    choose = jnp.where(in_pair, 1.0, 0.0)
    pair_lane = lax.broadcasted_iota(jnp.int32, (1, wide), 1) // npno
    filled = jnp.zeros((1, wide), jnp.float32)
    for n in range(pairs):
        both_occupied = (
            occupied[aux * 16 + pair_orbs[0, n]] + occupied[aux * 16 + pair_orbs[1, n]]
        )
        filled = jnp.where(pair_lane == n, both_occupied, filled)
    down, along_lanes = [], []
    for k in range(2):
        level = levels[:, k, :]
        down.append(
            lax.dot_general(
                level, choose, (((0,), (0,)), ((), ())), precision=EXACT,
                preferred_element_type=jnp.float32,
            )
        )
        every = jnp.dot(level, repeat, precision=EXACT, preferred_element_type=jnp.float32)
        along_lanes.append(jnp.sum(jnp.where(in_pair, every, 0.0), axis=0, keepdims=True))
    gap[0] = down[0] + along_lanes[1] - filled
    gap[1] = down[1] + along_lanes[0] - filled

    load_inverse.wait()
    own_offset = offsets[aux * 16 + orb]
    tile = 256

    def turn(n, carry):
        start = pl.multiple_of(n * tile, tile)
        to_row = lax.broadcasted_iota(jnp.int32, (tile, fit), 0) + start
        from_row = lax.broadcasted_iota(jnp.int32, (tile, fit), 1)
        hit = jnp.bitwise_and(to_row - from_row - own_offset + 2 * fit, fit - 1) == 0
        pick = jnp.where(hit, 1.0, 0.0).astype(jnp.bfloat16)
        rolled[pl.ds(start, tile), :] = jnp.dot(
            pick, inverse[...], preferred_element_type=jnp.float32
        ).astype(jnp.bfloat16)
        return carry

    lax.fori_loop(0, fit // tile, turn, 0)

    unread = []
    for da in HOPS:
        told[da].wait_recv()
        unread.append(
            pltpu.make_async_copy(notes.at[da - 1], notices.at[da - 1], note_sem.at[da - 1])
        )
        unread[-1].start()
    flags_out[0] = jnp.maximum(
        jnp.maximum(notes[0], notes[1]), jnp.maximum(notes[2], note[...])
    )
    flag_copies = []
    for db in HOPS:
        flag_copies.append(
            pltpu.make_async_remote_copy(
                src_ref=flags_out.at[0], dst_ref=flags_across.at[db - 1],
                send_sem=across_send.at[db - 1], recv_sem=across_recv.at[db - 1],
                device_id=(aux, turned(0, db)), device_id_type=MESH,
            )
        )
        flag_copies[-1].start()
    for copy in unread:
        copy.wait()

    for da in (2, 1, 3):
        first[da].wait_recv()
        for db in (1, 3, 2, 0):
            base = turned(0, db) * CAP
            for j in range(CAP):
                away[da, db, j] = mid[da][notices[da - 1, 0, base + j]]
            if db != 0:
                send_second(da, db)

    for copy in flag_copies:
        copy.wait()
    flags_out[1] = jnp.maximum(
        jnp.maximum(flags_across[0], flags_across[1]),
        jnp.maximum(flags_across[2], flags_out[0]),
    )
    last_flags = []
    for i, hop in enumerate(RAW_HOPS):
        last_flags.append(
            pltpu.make_async_remote_copy(
                src_ref=flags_out.at[1], dst_ref=flags_aux.at[i],
                send_sem=aux_send.at[i], recv_sem=aux_recv.at[i],
                device_id=(raw_peer(*hop), orb), device_id_type=MESH,
            )
        )
        last_flags[-1].start()

    load_own.wait()
    for copy in raw_copies:
        copy.wait_recv()

    def fit_tile(n, carry):
        start = pl.multiple_of(n * tile, tile)
        block = jnp.dot(
            rolled[...], gathered[:, pl.ds(start, tile)], preferred_element_type=jnp.float32
        ).astype(jnp.bfloat16)
        fitted_t[pl.ds(start, tile), :] = block.T
        return carry

    lax.fori_loop(0, dom // tile, fit_tile, 0)

    def project(source, target):
        def columns(n, carry):
            start = pl.multiple_of(n * tile, tile)
            lhs = source[...].reshape(CAP * npno, dom)
            block = jnp.dot(
                lhs, fitted_t[:, pl.ds(start, tile)], preferred_element_type=jnp.float32
            ).astype(jnp.bfloat16)
            target[:, :, pl.ds(start, tile)] = block.reshape(CAP, npno, tile)
            return carry

        lax.fori_loop(0, fit // tile, columns, 0)

    for da in HOPS:
        project(away.at[da, 0], back[da].at[pl.ds(0, CAP)])
    project(away.at[0, 0], home.at[pl.ds(0, CAP)])
    for db in HOPS:
        second[0, db].wait_recv()
        project(last.at[0, db - 1], sides.at[0, db - 1])
    relays = (2, 1, 3)
    for i, da in enumerate(relays):
        for k, db in enumerate(HOPS):
            second[da, db].wait_recv()
            project(last.at[da, db - 1], sides.at[da, db - 1])
            send_third(da, db)
            if i > 0 and k == 2:
                send_fourth(relays[i - 1])
    for db in HOPS:
        send_third(0, db)
    if 2 > 2:
        send_fourth(relays[0])
        send_fourth(relays[1])
    send_fourth(relays[2])
    for db in HOPS:
        third[0, db].wait_recv()
    for da in HOPS:
        fourth[da].wait_recv()

    per = tile // npno
    lanes = 128
    packed = lanes // npno
    fit_lane = lax.broadcasted_iota(jnp.int32, (npno, fit), 1)
    block_of = lax.broadcasted_iota(jnp.int32, (npno, lanes), 1) // npno
    contract = (((1,), (1,)), ((), ()))
    energies = jnp.zeros((1, lanes), jnp.float32)
    one_lane = lax.broadcasted_iota(jnp.int32, (1, lanes), 1)
    for half in range(pairs // per):
        for i in range(per):
            n = half * per + i
            off_0 = offsets[aux * 16 + pair_orbs[0, n]]
            off_1 = offsets[aux * 16 + pair_orbs[1, n]]
            low, high = jnp.minimum(off_0, off_1), jnp.maximum(off_0, off_1)
            one = home[lookup[1, 2 * n]]
            outside = jnp.logical_and(fit_lane >= low, fit_lane < high)
            left[pl.ds(i * npno, npno), :] = jnp.where(outside, jnp.zeros_like(one), one)
            right[pl.ds(i * npno, npno), :] = home[lookup[1, 2 * n + 1]]
        ahead = lax.dot_general(
            left[...], right[...], contract, preferred_element_type=jnp.float32
        )
        behind = lax.dot_general(
            right[...], left[...], contract, preferred_element_type=jnp.float32
        )
        for part in range(per // packed):
            forward = jnp.zeros((npno, lanes), jnp.float32)
            swapped = jnp.zeros((npno, lanes), jnp.float32)
            for i in range(packed):
                at = (part * packed + i) * npno
                here = block_of == i
                cut = slice(part * lanes, (part + 1) * lanes)
                forward = jnp.where(here, ahead[at:at + npno, cut], forward)
                swapped = jnp.where(here, behind[at:at + npno, cut], swapped)
            first_pair = half * per + part * packed
            span = pl.ds(first_pair * npno, lanes)
            amplitude = -forward / gap[0, :, span]
            mirrored = -swapped / gap[1, :, span]
            share = jnp.sum(
                forward * (2.0 * amplitude - mirrored), axis=0, keepdims=True
            )
            for shift in (1, 2, 4, 8, 16):
                share = share + pltpu.roll(share, lanes - shift, 1)
            for i in range(packed):
                n = first_pair + i
                energies = jnp.where(
                    one_lane == n, pltpu.roll(share, (n - i * npno) % lanes, 1), energies
                )
            spread[...] = amplitude
            strided = [spread[pl.ds(u, npno // packed, stride=packed), :] for u in range(packed)]
            for i in range(packed):
                line = jnp.zeros((npno // packed, lanes), jnp.float32)
                for u in range(packed):
                    moved = pltpu.roll(strided[u], ((u - i) * npno) % lanes, 1)
                    line = jnp.where(block_of[:npno // packed] == u, moved, line)
                n = first_pair + i
                for t in range(npno // packed):
                    out_ref[n:n + 1, t * lanes:(t + 1) * lanes] = line[t:t + 1]
    energy_ref[...] = energies
    every_flag = flags_out[1]
    for i, copy in enumerate(last_flags):
        copy.wait()
        every_flag = jnp.maximum(every_flag, flags_aux[i])
    crowded_ref[0] = jnp.max(every_flag[2:3])

    for copy in raw_copies:
        copy.wait_send()
    for group in (told, first, second, third, fourth):
        for copy in group.values():
            copy.wait_send()


def align_rows(shifted_in, begin_at):
    return lax.dynamic_slice_in_dim(shifted_in, begin_at, shifted_in.shape[1] * 2 // 3, 1)


def spread_out(raw_ints, fit_inverse, pair_orbs, pno_coef, pno_energy, occ_energy, fit_offset):
    orb_count = lax.axis_size("orb")
    region = lax.axis_index("aux")
    inverse = fit_inverse[0]
    gathered = lax.all_to_all(raw_ints, "aux", split_axis=0, concat_axis=2, tiled=True)
    fitted = jnp.dot(inverse, gathered[0, 0], preferred_element_type=jnp.float32).astype(
        jnp.bfloat16
    )
    fit_rows = fitted.shape[0]
    pair_count = pair_orbs.shape[0]
    pno_count = pno_coef.shape[2]
    dom_count = pno_coef.shape[3]
    side_count = 2 * pair_count
    capacity = max(2, 4 * pair_count // orb_count)
    slot_count = orb_count * capacity
    side_orbs = pair_orbs.reshape(side_count)
    matches = side_orbs[:, None] == side_orbs[None, :]
    sequence = jnp.arange(side_count, dtype=jnp.int32)
    earlier = sequence[None, :] < sequence[:, None]
    position = jnp.sum(jnp.where(matches & earlier, 1, 0), axis=1)
    slot_index = side_orbs * capacity + position
    placing = jnp.where(
        slot_index[None, :] == jnp.arange(slot_count, dtype=jnp.int32)[:, None], 1.0, 0.0
    ).astype(jnp.bfloat16)
    outgoing = jnp.dot(
        placing,
        pno_coef.reshape(side_count, pno_count * dom_count),
        preferred_element_type=jnp.float32,
    ).astype(jnp.bfloat16)
    outgoing = outgoing.reshape(orb_count, capacity, pno_count, dom_count)
    projected = jnp.einsum(
        "scpd,fd->scpf",
        lax.all_to_all(outgoing, "orb", split_axis=0, concat_axis=0, tiled=True),
        fitted,
        preferred_element_type=jnp.float32,
    ).astype(jnp.bfloat16)
    returned = lax.all_to_all(projected, "orb", split_axis=0, concat_axis=0, tiled=True)
    side_blocks = jnp.dot(
        placing.T,
        returned.reshape(slot_count, pno_count * fit_rows),
        preferred_element_type=jnp.float32,
    ).astype(jnp.bfloat16)
    side_blocks = side_blocks.reshape(pair_count, 2, pno_count, fit_rows)
    orb_total = occ_energy.shape[0]
    global_orb = region * orb_count + pair_orbs
    selector = global_orb[:, :, None] == jnp.arange(orb_total, dtype=jnp.int32)[None, None, :]
    offsets = jnp.sum(jnp.where(selector, fit_offset[None, None, :], 0), axis=2)
    occupied = jnp.sum(jnp.where(selector, occ_energy[None, None, :], 0.0), axis=2)
    margin = fit_rows // 4
    shift_rows = offsets[:, 0] - offsets[:, 1]
    padded = jnp.pad(side_blocks[:, 1], ((0, 0), (0, 0), (margin, margin)))
    aligned = jax.vmap(align_rows)(padded, margin + shift_rows)
    coupling = jnp.einsum(
        "npr,nqr->npq", side_blocks[:, 0], aligned, preferred_element_type=jnp.float32
    )
    denominator = (
        pno_energy[:, 0, :, None]
        + pno_energy[:, 1, None, :]
        - occupied[:, 0, None, None]
        - occupied[:, 1, None, None]
    )
    amplitude = -coupling / denominator
    energy = jnp.sum(coupling * (2.0 * amplitude - jnp.swapaxes(amplitude, 1, 2)), axis=(1, 2))
    return (amplitude.reshape(pair_count, pno_count * pno_count), energy)


def on_device(raw_ints, fit_inverse, pair_orbs, pno_coef, pno_energy, occ_energy, fit_offset):
    pairs, _, npno, dom = pno_coef.shape
    fit = fit_inverse.shape[1]
    bf16 = jnp.bfloat16
    f32 = jnp.float32
    i32 = jnp.int32
    vmem = pltpu.VMEM
    dma = pltpu.SemaphoreType.DMA
    smem_spec = pl.BlockSpec(memory_space=pltpu.SMEM)
    vmem_spec = pl.BlockSpec(memory_space=pltpu.VMEM)
    any_spec = pl.BlockSpec(memory_space=pl.ANY)
    amplitude, energy, crowded = pl.pallas_call(
        exchange_kernel,
        out_shape=(
            jax.ShapeDtypeStruct((pairs, npno * npno), f32),
            jax.ShapeDtypeStruct((1, 128), f32),
            jax.ShapeDtypeStruct((1,), i32),
        ),
        in_specs=[smem_spec] * 3 + [vmem_spec] + [any_spec] * 3,
        out_specs=(vmem_spec, vmem_spec, smem_spec),
        scratch_shapes=[
            vmem((2 * pairs, npno, dom), bf16),
            vmem((fit, fit), bf16),
            vmem((fit, fit), bf16),
            vmem((fit, dom), bf16),
            vmem((dom, fit), bf16),
            vmem((3, ROW, npno, dom), bf16),
            vmem((ROW, npno, dom), bf16),
            vmem((ROW, npno, dom), bf16),
            vmem((ROW, npno, dom), bf16),
            vmem((4, 4, CAP, npno, dom), bf16),
            vmem((4, 3, CAP, npno, dom), bf16),
            vmem((4, 3, CAP, npno, fit), bf16),
            vmem((4 * CAP, npno, fit), bf16),
            vmem((4 * CAP, npno, fit), bf16),
            vmem((4 * CAP, npno, fit), bf16),
            vmem((3, ROW, npno, fit), bf16),
            vmem((4 * CAP + 3 * ROW, npno, fit), bf16),
            vmem((256, fit), bf16),
            vmem((256, fit), bf16),
            vmem((2, npno, pairs * npno), f32),
            vmem((npno, 128), f32),
            vmem((8, 128), i32),
            vmem((8, 128), i32),
            vmem((3, 8, 128), i32),
            vmem((2, 8, 128), i32),
            vmem((3, 8, 128), i32),
            vmem((7, 8, 128), i32),
            pltpu.SMEM((8, 128), i32),
            pltpu.SMEM((3, 8, 128), i32),
            dma((4,)), dma((7,)), dma((7,)),
            dma((3,)), dma((3,)), dma((12,)), dma((12,)),
            dma((12,)), dma((12,)), dma((3,)), dma((3,)),
            dma((3,)), dma((3,)), dma((3,)),
            dma((3,)), dma((3,)), dma((7,)), dma((7,)),
        ],
        compiler_params=pltpu.CompilerParams(
            collective_id=0, has_side_effects=True, vmem_limit_bytes=58 * 2**20
        ),
        name="exchange",
    )(
        pair_orbs.T, fit_offset, occ_energy, pno_energy,
        raw_ints, fit_inverse, pno_coef.reshape(2 * pairs, npno, dom),
    )
    return lax.cond(
        crowded[0] > 0,
        lambda: spread_out(
            raw_ints, fit_inverse, pair_orbs, pno_coef, pno_energy, occ_energy, fit_offset
        ),
        lambda: (amplitude, energy[0, :pairs]),
    )


def solution(mesh):
    return jax.shard_map(
        on_device,
        mesh=mesh,
        in_specs=(
            P(None, "orb", "aux", None),
            P(("aux", "orb"), None, None),
            P(("aux", "orb"), None),
            P(("aux", "orb"), None, None, None),
            P(("aux", "orb"), None, None),
            P(),
            P(),
        ),
        out_specs=(P(("aux", "orb"), None), P(("aux", "orb"))),
        check_vma=False,
    )
```

```python
import jax
import jax.numpy as jnp
from jax import lax
from jax.experimental import pallas as pl
from jax.experimental.pallas import tpu as pltpu
from jax.sharding import PartitionSpec as P

MESH = pl.DeviceIdType.MESH
HOPS = (1, 3, 2)
RAW_HOPS = ((0, 1), (1, 0), (3, 0), (1, 1), (3, 1), (2, 0), (2, 1))
CAP = 4
ROW = 11
BLOCK = 512
EXACT = lax.Precision.HIGHEST


def exchange_kernel(
    pair_orbs, offsets, occupied, levels, raw_ref, inv_ref, coef_ref,
    out_ref, energy_ref, crowded_ref,
    coef, inverse, rolled, gathered, fitted, packed_out, mid_1, mid_2, mid_3, away,
    back_1, back_2, back_3, packed_back, home,
    left, right, inside, gap, spread, table, note, notes, flags_out, flags_across, flags_aux,
    lookup, notices,
    local_sem, raw_send, raw_recv, p1_send, p1_recv, fit_send, fit_recv,
    pass_send, pass_recv, r2_send, r2_recv, note_send, note_recv, note_sem,
    across_send, across_recv, aux_send, aux_recv,
):
    mid = {1: mid_1, 2: mid_2, 3: mid_3}
    back = {1: back_1, 2: back_2, 3: back_3}
    aux = lax.axis_index("aux")
    orb = lax.axis_index("orb")
    x, core = aux // 2, lax.rem(aux, 2)
    y, z = orb // 4, lax.rem(orb, 4)
    fit = inverse.shape[0]
    dom = fitted.shape[1]
    blocks = dom // BLOCK
    side_count, npno, _ = coef.shape
    pairs = side_count // 2
    rows = raw_ref.shape[2]

    def turned(d_first, d_second):
        dy = jnp.where(core == 0, d_first, d_second)
        dz = jnp.where(core == 0, d_second, d_first)
        return lax.rem(y + dy, 4) * 4 + lax.rem(z + dz, 4)

    def raw_peer(dx, dc):
        return lax.rem(x + dx, 4) * 2 + lax.rem(core + dc, 2)

    load_coef = pltpu.make_async_copy(coef_ref, coef, local_sem.at[0])
    load_inverse = pltpu.make_async_copy(inv_ref.at[0], inverse, local_sem.at[1])
    load_own = pltpu.make_async_copy(
        raw_ref.at[aux, 0], gathered.at[pl.ds(aux * rows, rows)], local_sem.at[2]
    )
    load_coef.start()
    load_inverse.start()
    load_own.start()

    barrier = pltpu.get_barrier_semaphore()
    for d in HOPS:
        pl.semaphore_signal(barrier, 1, device_id=(aux, turned(d, 0)), device_id_type=MESH)
        pl.semaphore_signal(barrier, 1, device_id=(aux, turned(0, d)), device_id_type=MESH)
    for hop in RAW_HOPS:
        pl.semaphore_signal(barrier, 1, device_id=(raw_peer(*hop), orb), device_id_type=MESH)

    own_along = jnp.where(core == 0, y, z)
    own_across = jnp.where(core == 0, z, y)

    def row_of(p):
        return jnp.where(core == 0, p // 4, jnp.bitwise_and(p, 3))

    def place_in_row(p):
        return jnp.where(core == 0, jnp.bitwise_and(p, 3), p // 4)

    lane = lax.broadcasted_iota(jnp.int32, (8, 128), 1)
    slot_orb, slot_place = lane // CAP, jnp.bitwise_and(lane, CAP - 1)
    slot_row = row_of(slot_orb)
    list_row, list_place = lane // 16, jnp.bitwise_and(lane, 15)
    zero = jnp.zeros((8, 128), jnp.int32)
    in_slot, in_list, list_orb, slot_list = zero, zero, zero, zero
    seen, seen_row, seen_list, own_orb = zero, zero, zero, zero
    for i in range(side_count):
        name = pair_orbs[i % 2, i // 2]
        row = row_of(name)
        match = slot_orb == name
        hit = jnp.logical_and(match, seen == slot_place)
        in_slot = jnp.where(hit, i, in_slot)
        slot_list = jnp.where(hit, seen_row, slot_list)
        seen = seen + jnp.where(match, 1, 0)
        seen_row = seen_row + jnp.where(slot_row == row, 1, 0)
        match = list_row == row
        hit = jnp.logical_and(match, seen_list == list_place)
        in_list = jnp.where(hit, i, in_list)
        list_orb = jnp.where(hit, name, list_orb)
        seen_list = seen_list + jnp.where(match, 1, 0)
        own_orb = jnp.where(lane == i, name, own_orb)
    own_row = row_of(own_orb)
    side_place, side_list, list_spot = zero, zero, zero
    for i in range(side_count):
        name = pair_orbs[i % 2, i // 2]
        after = lane > i
        side_place = side_place + jnp.where(jnp.logical_and(own_orb == name, after), 1, 0)
        side_list = side_list + jnp.where(
            jnp.logical_and(own_row == row_of(name), after), 1, 0
        )
        list_spot = list_spot + jnp.where(
            jnp.logical_and(list_orb == name, in_list > i), 1, 0
        )
    along = jnp.bitwise_and(own_row + 4 - own_along, 3)
    across = jnp.bitwise_and(place_in_row(own_orb) + 4 - own_across, 3)
    home_slot = jnp.where(
        along == 0,
        across * CAP + jnp.minimum(side_place, CAP - 1),
        4 * CAP + (along - 1) * ROW + jnp.minimum(side_list, ROW - 1),
    )
    list_slot = (
        jnp.bitwise_and(place_in_row(list_orb) + 4 - own_across, 3) * CAP
        + jnp.minimum(list_spot, CAP - 1)
    )
    crowded = jnp.max(jnp.where(jnp.logical_and(list_row < 4, seen_list > ROW), 1, 0))
    row_at = lax.broadcasted_iota(jnp.int32, (8, 128), 0)
    table[...] = jnp.where(row_at == 0, in_slot, jnp.where(row_at == 1, home_slot, in_list))
    note[...] = jnp.where(
        row_at == 0,
        jnp.minimum(slot_list, ROW - 1),
        jnp.where(row_at == 1, list_slot, crowded),
    )
    load_table = pltpu.make_async_copy(table, lookup, local_sem.at[3])
    load_table.start()

    pl.semaphore_wait(barrier, 2 * len(HOPS) + len(RAW_HOPS))
    raw_copies = {}

    def send_raw(b):
        columns = pl.ds(b * BLOCK, BLOCK)
        for i, hop in enumerate(RAW_HOPS):
            peer = raw_peer(*hop)
            raw_copies[b, i] = pltpu.make_async_remote_copy(
                src_ref=raw_ref.at[peer, 0, :, columns],
                dst_ref=gathered.at[pl.ds(aux * rows, rows), columns],
                send_sem=raw_send.at[b * len(RAW_HOPS) + i],
                recv_sem=raw_recv.at[b * len(RAW_HOPS) + i],
                device_id=(peer, orb),
                device_id_type=MESH,
            )
            raw_copies[b, i].start()

    send_raw(0)
    told, first, fourth, shown, passed = {}, {}, {}, {}, {}

    def tell(da):
        told[da] = pltpu.make_async_remote_copy(
            src_ref=note, dst_ref=notes.at[da - 1],
            send_sem=note_send.at[da - 1], recv_sem=note_recv.at[da - 1],
            device_id=(aux, turned(da, 0)), device_id_type=MESH,
        )
        told[da].start()

    def send_first(da):
        first[da] = pltpu.make_async_remote_copy(
            src_ref=packed_out.at[da - 1], dst_ref=mid[da],
            send_sem=p1_send.at[da - 1], recv_sem=p1_recv.at[da - 1],
            device_id=(aux, turned(da, 0)), device_id_type=MESH,
        )
        first[da].start()

    def show(b):
        span = pl.ds(b * BLOCK, BLOCK)
        for k, db in enumerate((1, 3)):
            shown[b, db] = pltpu.make_async_remote_copy(
                src_ref=fitted.at[0, span], dst_ref=fitted.at[4 - db, span],
                send_sem=fit_send.at[2 * b + k], recv_sem=fit_recv.at[2 * b + k],
                device_id=(aux, turned(0, db)), device_id_type=MESH,
            )
            shown[b, db].start()

    def pass_on(b):
        for k, db in enumerate((1, 3)):
            shown[b, db].wait_recv()
            span = pl.ds(b * BLOCK + k * (BLOCK // 2), BLOCK // 2)
            passed[b, db] = pltpu.make_async_remote_copy(
                src_ref=fitted.at[4 - db, span], dst_ref=fitted.at[2, span],
                send_sem=pass_send.at[2 * b + k], recv_sem=pass_recv.at[2 * b + k],
                device_id=(aux, turned(0, db)), device_id_type=MESH,
            )
            passed[b, db].start()

    def send_fourth(da):
        at = (own_along * 16)
        for q in range(ROW):
            packed_back[da - 1, q] = back[da][notices[da - 1, 1, at + q]]
        fourth[da] = pltpu.make_async_remote_copy(
            src_ref=packed_back.at[da - 1],
            dst_ref=home.at[pl.ds(4 * CAP + (da - 1) * ROW, ROW)],
            send_sem=r2_send.at[da - 1], recv_sem=r2_recv.at[da - 1],
            device_id=(aux, turned(4 - da, 0)), device_id_type=MESH,
        )
        fourth[da].start()

    for da in HOPS:
        tell(da)
    load_coef.wait()
    load_table.wait()
    for da in (2, 1, 3):
        to_row = jnp.bitwise_and(own_along + da, 3) * 16
        for q in range(ROW):
            packed_out[da - 1, q] = coef[lookup[2, to_row + q]]
        send_first(da)
    for db in range(4):
        base = turned(0, db) * CAP
        for j in range(CAP):
            away[0, db, j] = coef[lookup[0, base + j]]
    if blocks > 1:
        send_raw(1)

    wide = pairs * npno
    of_lane = lax.broadcasted_iota(jnp.int32, (pairs, wide), 1) // npno
    in_pair = of_lane == lax.broadcasted_iota(jnp.int32, (pairs, wide), 0)
    repeat = jnp.where(
        lax.broadcasted_iota(jnp.int32, (npno, wide), 0)
        == jnp.bitwise_and(lax.broadcasted_iota(jnp.int32, (npno, wide), 1), npno - 1),
        1.0, 0.0,
    )
    choose = jnp.where(in_pair, 1.0, 0.0)
    pair_lane = lax.broadcasted_iota(jnp.int32, (1, wide), 1) // npno
    filled = jnp.zeros((1, wide), jnp.float32)
    for n in range(pairs):
        both_occupied = (
            occupied[aux * 16 + pair_orbs[0, n]] + occupied[aux * 16 + pair_orbs[1, n]]
        )
        filled = jnp.where(pair_lane == n, both_occupied, filled)
    down, along_lanes = [], []
    for k in range(2):
        level = levels[:, k, :]
        down.append(
            lax.dot_general(
                level, choose, (((0,), (0,)), ((), ())), precision=EXACT,
                preferred_element_type=jnp.float32,
            )
        )
        every = jnp.dot(level, repeat, precision=EXACT, preferred_element_type=jnp.float32)
        along_lanes.append(jnp.sum(jnp.where(in_pair, every, 0.0), axis=0, keepdims=True))
    gap[0] = down[0] + along_lanes[1] - filled
    gap[1] = down[1] + along_lanes[0] - filled

    fit_lane = lax.broadcasted_iota(jnp.int32, (16, fit), 1)
    for n in range(pairs):
        off_0 = offsets[aux * 16 + pair_orbs[0, n]]
        off_1 = offsets[aux * 16 + pair_orbs[1, n]]
        low, high = jnp.minimum(off_0, off_1), jnp.maximum(off_0, off_1)
        outside = jnp.logical_and(fit_lane >= low, fit_lane < high)
        inside[n] = jnp.where(outside, 0.0, 1.0).astype(jnp.bfloat16)

    load_inverse.wait()
    own_offset = offsets[aux * 16 + orb]
    tile = 256

    def turn(n, carry):
        start = pl.multiple_of(n * tile, tile)
        to_row = lax.broadcasted_iota(jnp.int32, (tile, fit), 0) + start
        from_row = lax.broadcasted_iota(jnp.int32, (tile, fit), 1)
        hit = jnp.bitwise_and(to_row - from_row - own_offset + 2 * fit, fit - 1) == 0
        pick = jnp.where(hit, 1.0, 0.0).astype(jnp.bfloat16)
        rolled[pl.ds(start, tile), :] = jnp.dot(
            pick, inverse[...], preferred_element_type=jnp.float32
        ).astype(jnp.bfloat16)
        return carry

    lax.fori_loop(0, fit // tile, turn, 0)

    unread = []
    for da in HOPS:
        told[da].wait_recv()
        unread.append(
            pltpu.make_async_copy(notes.at[da - 1], notices.at[da - 1], note_sem.at[da - 1])
        )
        unread[-1].start()
    flags_out[0] = jnp.maximum(
        jnp.maximum(notes[0], notes[1]), jnp.maximum(notes[2], note[...])
    )
    flag_copies = []
    for db in HOPS:
        flag_copies.append(
            pltpu.make_async_remote_copy(
                src_ref=flags_out.at[0], dst_ref=flags_across.at[db - 1],
                send_sem=across_send.at[db - 1], recv_sem=across_recv.at[db - 1],
                device_id=(aux, turned(0, db)), device_id_type=MESH,
            )
        )
        flag_copies[-1].start()
    for copy in unread:
        copy.wait()

    for copy in flag_copies:
        copy.wait()
    flags_out[1] = jnp.maximum(
        jnp.maximum(flags_across[0], flags_across[1]),
        jnp.maximum(flags_across[2], flags_out[0]),
    )
    last_flags = []
    for i, hop in enumerate(RAW_HOPS):
        last_flags.append(
            pltpu.make_async_remote_copy(
                src_ref=flags_out.at[1], dst_ref=flags_aux.at[i],
                send_sem=aux_send.at[i], recv_sem=aux_recv.at[i],
                device_id=(raw_peer(*hop), orb), device_id_type=MESH,
            )
        )
        last_flags[-1].start()

    load_own.wait()
    for b in range(blocks):
        for i in range(len(RAW_HOPS)):
            raw_copies[b, i].wait_recv()
        if b + 2 < blocks:
            send_raw(b + 2)

        def fit_tile(n, carry):
            start = pl.multiple_of(b * BLOCK + n * tile, tile)
            block = jnp.dot(
                rolled[...], gathered[:, pl.ds(start, tile)],
                preferred_element_type=jnp.float32,
            ).astype(jnp.bfloat16)
            fitted[0, pl.ds(start, tile), :] = block.T
            return carry

        lax.fori_loop(0, BLOCK // tile, fit_tile, 0)
        show(b)
        if b > 0:
            pass_on(b - 1)

    for da in (2, 1, 3):
        first[da].wait_recv()
        for db in range(4):
            base = turned(0, db) * CAP
            for j in range(CAP):
                away[da, db, j] = mid[da][notices[da - 1, 0, base + j]]

    def project(source, db, target):
        def columns(n, carry):
            start = pl.multiple_of(n * tile, tile)
            lhs = source[...].reshape(CAP * npno, dom)
            block = jnp.dot(
                lhs, fitted[db, :, pl.ds(start, tile)], preferred_element_type=jnp.float32
            ).astype(jnp.bfloat16)
            target[:, :, pl.ds(start, tile)] = block.reshape(CAP, npno, tile)
            return carry

        lax.fori_loop(0, fit // tile, columns, 0)

    def project_all(da, db):
        spots = pl.ds(db * CAP, CAP)
        project(away.at[da, db], db, home.at[spots] if da == 0 else back[da].at[spots])

    everyone = (2, 1, 3, 0)
    for da in everyone[:2]:
        project_all(da, 0)
    pass_on(blocks - 1)
    for da in everyone[2:]:
        project_all(da, 0)
    for db in (1, 3):
        for da in everyone:
            project_all(da, db)
    for copy in passed.values():
        copy.wait_recv()
    for da in everyone:
        project_all(da, 2)
        if da != 0:
            send_fourth(da)
    for da in HOPS:
        fourth[da].wait_recv()

    per = tile // npno
    lanes = 128
    packed = lanes // npno
    block_of = lax.broadcasted_iota(jnp.int32, (npno, lanes), 1) // npno
    contract = (((1,), (1,)), ((), ()))
    energies = jnp.zeros((1, lanes), jnp.float32)
    one_lane = lax.broadcasted_iota(jnp.int32, (1, lanes), 1)
    for half in range(pairs // per):
        for i in range(per):
            n = half * per + i
            one = home[lookup[1, 2 * n]]
            for part in range(npno // 16):
                left[pl.ds(i * npno + part * 16, 16), :] = (
                    one[part * 16:(part + 1) * 16] * inside[n]
                )
            right[pl.ds(i * npno, npno), :] = home[lookup[1, 2 * n + 1]]
        ahead = lax.dot_general(
            left[...], right[...], contract, preferred_element_type=jnp.float32
        )
        behind = ahead.T
        for part in range(per // packed):
            forward = jnp.zeros((npno, lanes), jnp.float32)
            swapped = jnp.zeros((npno, lanes), jnp.float32)
            for i in range(packed):
                at = (part * packed + i) * npno
                here = block_of == i
                cut = slice(part * lanes, (part + 1) * lanes)
                forward = jnp.where(here, ahead[at:at + npno, cut], forward)
                swapped = jnp.where(here, behind[at:at + npno, cut], swapped)
            first_pair = half * per + part * packed
            span = pl.ds(first_pair * npno, lanes)
            amplitude = -forward / gap[0, :, span]
            mirrored = -swapped / gap[1, :, span]
            share = jnp.sum(
                forward * (2.0 * amplitude - mirrored), axis=0, keepdims=True
            )
            for shift in (1, 2, 4, 8, 16):
                share = share + pltpu.roll(share, lanes - shift, 1)
            for i in range(packed):
                n = first_pair + i
                energies = jnp.where(
                    one_lane == n, pltpu.roll(share, (n - i * npno) % lanes, 1), energies
                )
            spread[...] = amplitude
            strided = [spread[pl.ds(u, npno // packed, stride=packed), :] for u in range(packed)]
            for i in range(packed):
                line = jnp.zeros((npno // packed, lanes), jnp.float32)
                for u in range(packed):
                    moved = pltpu.roll(strided[u], ((u - i) * npno) % lanes, 1)
                    line = jnp.where(block_of[:npno // packed] == u, moved, line)
                n = first_pair + i
                for t in range(npno // packed):
                    out_ref[n:n + 1, t * lanes:(t + 1) * lanes] = line[t:t + 1]
    energy_ref[...] = energies
    every_flag = flags_out[1]
    for i, copy in enumerate(last_flags):
        copy.wait()
        every_flag = jnp.maximum(every_flag, flags_aux[i])
    crowded_ref[0] = jnp.max(every_flag[2:3])

    for group in (raw_copies, told, first, shown, passed, fourth):
        for copy in group.values():
            copy.wait_send()


def align_rows(shifted_in, begin_at):
    return lax.dynamic_slice_in_dim(shifted_in, begin_at, shifted_in.shape[1] * 2 // 3, 1)


def spread_out(raw_ints, fit_inverse, pair_orbs, pno_coef, pno_energy, occ_energy, fit_offset):
    orb_count = lax.axis_size("orb")
    region = lax.axis_index("aux")
    inverse = fit_inverse[0]
    gathered = lax.all_to_all(raw_ints, "aux", split_axis=0, concat_axis=2, tiled=True)
    fitted = jnp.dot(inverse, gathered[0, 0], preferred_element_type=jnp.float32).astype(
        jnp.bfloat16
    )
    fit_rows = fitted.shape[0]
    pair_count = pair_orbs.shape[0]
    pno_count = pno_coef.shape[2]
    dom_count = pno_coef.shape[3]
    side_count = 2 * pair_count
    capacity = max(2, 4 * pair_count // orb_count)
    slot_count = orb_count * capacity
    side_orbs = pair_orbs.reshape(side_count)
    matches = side_orbs[:, None] == side_orbs[None, :]
    sequence = jnp.arange(side_count, dtype=jnp.int32)
    earlier = sequence[None, :] < sequence[:, None]
    position = jnp.sum(jnp.where(matches & earlier, 1, 0), axis=1)
    slot_index = side_orbs * capacity + position
    placing = jnp.where(
        slot_index[None, :] == jnp.arange(slot_count, dtype=jnp.int32)[:, None], 1.0, 0.0
    ).astype(jnp.bfloat16)
    outgoing = jnp.dot(
        placing,
        pno_coef.reshape(side_count, pno_count * dom_count),
        preferred_element_type=jnp.float32,
    ).astype(jnp.bfloat16)
    outgoing = outgoing.reshape(orb_count, capacity, pno_count, dom_count)
    projected = jnp.einsum(
        "scpd,fd->scpf",
        lax.all_to_all(outgoing, "orb", split_axis=0, concat_axis=0, tiled=True),
        fitted,
        preferred_element_type=jnp.float32,
    ).astype(jnp.bfloat16)
    returned = lax.all_to_all(projected, "orb", split_axis=0, concat_axis=0, tiled=True)
    side_blocks = jnp.dot(
        placing.T,
        returned.reshape(slot_count, pno_count * fit_rows),
        preferred_element_type=jnp.float32,
    ).astype(jnp.bfloat16)
    side_blocks = side_blocks.reshape(pair_count, 2, pno_count, fit_rows)
    orb_total = occ_energy.shape[0]
    global_orb = region * orb_count + pair_orbs
    selector = global_orb[:, :, None] == jnp.arange(orb_total, dtype=jnp.int32)[None, None, :]
    offsets = jnp.sum(jnp.where(selector, fit_offset[None, None, :], 0), axis=2)
    occupied = jnp.sum(jnp.where(selector, occ_energy[None, None, :], 0.0), axis=2)
    margin = fit_rows // 4
    shift_rows = offsets[:, 0] - offsets[:, 1]
    padded = jnp.pad(side_blocks[:, 1], ((0, 0), (0, 0), (margin, margin)))
    aligned = jax.vmap(align_rows)(padded, margin + shift_rows)
    coupling = jnp.einsum(
        "npr,nqr->npq", side_blocks[:, 0], aligned, preferred_element_type=jnp.float32
    )
    denominator = (
        pno_energy[:, 0, :, None]
        + pno_energy[:, 1, None, :]
        - occupied[:, 0, None, None]
        - occupied[:, 1, None, None]
    )
    amplitude = -coupling / denominator
    energy = jnp.sum(coupling * (2.0 * amplitude - jnp.swapaxes(amplitude, 1, 2)), axis=(1, 2))
    return (amplitude.reshape(pair_count, pno_count * pno_count), energy)


def on_device(raw_ints, fit_inverse, pair_orbs, pno_coef, pno_energy, occ_energy, fit_offset):
    pairs, _, npno, dom = pno_coef.shape
    fit = fit_inverse.shape[1]
    bf16 = jnp.bfloat16
    f32 = jnp.float32
    i32 = jnp.int32
    blocks = dom // BLOCK
    vmem = pltpu.VMEM
    dma = pltpu.SemaphoreType.DMA
    smem_spec = pl.BlockSpec(memory_space=pltpu.SMEM)
    vmem_spec = pl.BlockSpec(memory_space=pltpu.VMEM)
    any_spec = pl.BlockSpec(memory_space=pl.ANY)
    amplitude, energy, crowded = pl.pallas_call(
        exchange_kernel,
        out_shape=(
            jax.ShapeDtypeStruct((pairs, npno * npno), f32),
            jax.ShapeDtypeStruct((1, 128), f32),
            jax.ShapeDtypeStruct((1,), i32),
        ),
        in_specs=[smem_spec] * 3 + [vmem_spec] + [any_spec] * 3,
        out_specs=(vmem_spec, vmem_spec, smem_spec),
        scratch_shapes=[
            vmem((2 * pairs, npno, dom), bf16),
            vmem((fit, fit), bf16),
            vmem((fit, fit), bf16),
            vmem((fit, dom), bf16),
            vmem((4, dom, fit), bf16),
            vmem((3, ROW, npno, dom), bf16),
            vmem((ROW, npno, dom), bf16),
            vmem((ROW, npno, dom), bf16),
            vmem((ROW, npno, dom), bf16),
            vmem((4, 4, CAP, npno, dom), bf16),
            vmem((4 * CAP, npno, fit), bf16),
            vmem((4 * CAP, npno, fit), bf16),
            vmem((4 * CAP, npno, fit), bf16),
            vmem((3, ROW, npno, fit), bf16),
            vmem((4 * CAP + 3 * ROW, npno, fit), bf16),
            vmem((256, fit), bf16),
            vmem((256, fit), bf16),
            vmem((pairs, 16, fit), bf16),
            vmem((2, npno, pairs * npno), f32),
            vmem((npno, 128), f32),
            vmem((8, 128), i32),
            vmem((8, 128), i32),
            vmem((3, 8, 128), i32),
            vmem((2, 8, 128), i32),
            vmem((3, 8, 128), i32),
            vmem((7, 8, 128), i32),
            pltpu.SMEM((8, 128), i32),
            pltpu.SMEM((3, 8, 128), i32),
            dma((4,)), dma((7 * blocks,)), dma((7 * blocks,)),
            dma((3,)), dma((3,)), dma((2 * blocks,)), dma((2 * blocks,)),
            dma((2 * blocks,)), dma((2 * blocks,)), dma((3,)), dma((3,)),
            dma((3,)), dma((3,)), dma((3,)),
            dma((3,)), dma((3,)), dma((7,)), dma((7,)),
        ],
        compiler_params=pltpu.CompilerParams(
            collective_id=0, has_side_effects=True, vmem_limit_bytes=58 * 2**20
        ),
        name="exchange",
    )(
        pair_orbs.T, fit_offset, occ_energy, pno_energy,
        raw_ints, fit_inverse, pno_coef.reshape(2 * pairs, npno, dom),
    )
    return lax.cond(
        crowded[0] > 0,
        lambda: spread_out(
            raw_ints, fit_inverse, pair_orbs, pno_coef, pno_energy, occ_energy, fit_offset
        ),
        lambda: (amplitude, energy[0, :pairs]),
    )


def solution(mesh):
    return jax.shard_map(
        on_device,
        mesh=mesh,
        in_specs=(
            P(None, "orb", "aux", None),
            P(("aux", "orb"), None, None),
            P(("aux", "orb"), None),
            P(("aux", "orb"), None, None, None),
            P(("aux", "orb"), None, None),
            P(),
            P(),
        ),
        out_specs=(P(("aux", "orb"), None), P(("aux", "orb"))),
        check_vma=False,
    )
```

```python
import jax
import jax.numpy as jnp
from jax import lax
from jax.experimental import pallas as pl
from jax.experimental.pallas import tpu as pltpu
from jax.sharding import PartitionSpec as P

MESH = pl.DeviceIdType.MESH
HOPS = (1, 3, 2)
RAW_HOPS = ((0, 1), (1, 0), (3, 0), (1, 1), (3, 1), (2, 0), (2, 1))
CAP = 4
ROW = 11
NEAR = 14
FAR = 6
FAR_AT = 1
BLOCK = 512
EXACT = lax.Precision.HIGHEST


def exchange_kernel(
    pair_orbs, offsets, occupied, levels, raw_ref, inv_ref, coef_ref,
    out_ref, energy_ref, crowded_ref,
    coef, inverse, rolled, gathered, fitted, packed_out, packed_far, mid_1, mid_2, mid_3, away,
    back_1, back_2, back_3, packed_back, home,
    left, right, inside, gap, spread, table, note, notes, flags_out, flags_across, flags_aux,
    lookup, notices,
    local_sem, raw_send, raw_recv, p1_send, p1_recv, fit_send, fit_recv,
    pass_send, pass_recv, r2_send, r2_recv, note_send, note_recv, note_sem,
    across_send, across_recv, aux_send, aux_recv,
):
    mid = {1: mid_1, 2: mid_2, 3: mid_3}
    back = {1: back_1, 2: back_2, 3: back_3}
    aux = lax.axis_index("aux")
    orb = lax.axis_index("orb")
    x, core = aux // 2, lax.rem(aux, 2)
    y, z = orb // 4, lax.rem(orb, 4)
    fit = inverse.shape[0]
    dom = fitted.shape[1]
    blocks = dom // BLOCK
    side_count, npno, _ = coef.shape
    pairs = side_count // 2
    rows = raw_ref.shape[2]

    def turned(d_first, d_second):
        dy = jnp.where(core == 0, d_first, d_second)
        dz = jnp.where(core == 0, d_second, d_first)
        return lax.rem(y + dy, 4) * 4 + lax.rem(z + dz, 4)

    def raw_peer(dx, dc):
        return lax.rem(x + dx, 4) * 2 + lax.rem(core + dc, 2)

    load_coef = pltpu.make_async_copy(coef_ref, coef, local_sem.at[0])
    load_inverse = pltpu.make_async_copy(inv_ref.at[0], inverse, local_sem.at[1])
    load_own = pltpu.make_async_copy(
        raw_ref.at[aux, 0], gathered.at[pl.ds(aux * rows, rows)], local_sem.at[2]
    )
    load_coef.start()
    load_inverse.start()
    load_own.start()

    barrier = pltpu.get_barrier_semaphore()
    for d in HOPS:
        pl.semaphore_signal(barrier, 1, device_id=(aux, turned(d, 0)), device_id_type=MESH)
        pl.semaphore_signal(barrier, 1, device_id=(aux, turned(0, d)), device_id_type=MESH)
    for hop in RAW_HOPS:
        pl.semaphore_signal(barrier, 1, device_id=(raw_peer(*hop), orb), device_id_type=MESH)

    own_along = jnp.where(core == 0, y, z)
    own_across = jnp.where(core == 0, z, y)

    def row_of(p):
        return jnp.where(core == 0, p // 4, jnp.bitwise_and(p, 3))

    def place_in_row(p):
        return jnp.where(core == 0, jnp.bitwise_and(p, 3), p // 4)

    lane = lax.broadcasted_iota(jnp.int32, (8, 128), 1)
    slot_orb, slot_place = lane // CAP, jnp.bitwise_and(lane, CAP - 1)
    slot_row = row_of(slot_orb)
    list_row, list_place = lane // 16, jnp.bitwise_and(lane, 15)
    zero = jnp.zeros((8, 128), jnp.int32)
    in_slot, in_list, list_orb, slot_list = zero, zero, zero, zero
    seen, seen_row, seen_list, own_orb = zero, zero, zero, zero
    for i in range(side_count):
        name = pair_orbs[i % 2, i // 2]
        row = row_of(name)
        match = slot_orb == name
        hit = jnp.logical_and(match, seen == slot_place)
        in_slot = jnp.where(hit, i, in_slot)
        slot_list = jnp.where(hit, seen_row, slot_list)
        seen = seen + jnp.where(match, 1, 0)
        seen_row = seen_row + jnp.where(slot_row == row, 1, 0)
        match = list_row == row
        hit = jnp.logical_and(match, seen_list == list_place)
        in_list = jnp.where(hit, i, in_list)
        list_orb = jnp.where(hit, name, list_orb)
        seen_list = seen_list + jnp.where(match, 1, 0)
        own_orb = jnp.where(lane == i, name, own_orb)
    own_row = row_of(own_orb)
    side_place, side_list, list_spot = zero, zero, zero
    for i in range(side_count):
        name = pair_orbs[i % 2, i // 2]
        after = lane > i
        side_place = side_place + jnp.where(jnp.logical_and(own_orb == name, after), 1, 0)
        side_list = side_list + jnp.where(
            jnp.logical_and(own_row == row_of(name), after), 1, 0
        )
        list_spot = list_spot + jnp.where(
            jnp.logical_and(list_orb == name, in_list > i), 1, 0
        )
    along = jnp.bitwise_and(own_row + 4 - own_along, 3)
    across = jnp.bitwise_and(place_in_row(own_orb) + 4 - own_across, 3)
    home_slot = jnp.where(
        along == 0,
        across * CAP + jnp.minimum(side_place, CAP - 1),
        4 * CAP + (along - 1) * ROW + jnp.minimum(side_list, ROW - 1),
    )
    list_slot = (
        jnp.bitwise_and(place_in_row(list_orb) + 4 - own_across, 3) * CAP
        + jnp.minimum(list_spot, CAP - 1)
    )
    def named(step):
        there = list_row == jnp.bitwise_and(own_along + step, 3)
        return jnp.max(jnp.where(there, seen_list, 0))

    ahead_count, far_count, behind_count = named(1), named(2), named(3)
    by_ahead = jnp.minimum(jnp.minimum(far_count, FAR), jnp.maximum(NEAR - ahead_count, 0))
    by_behind = far_count - by_ahead
    fits = jnp.logical_and(
        jnp.logical_and(ahead_count <= ROW, behind_count <= ROW),
        jnp.logical_and(
            far_count <= ROW,
            jnp.logical_and(by_behind <= FAR, behind_count + by_behind <= NEAR),
        ),
    )
    crowded = jnp.where(fits, 0, 1)
    in_far = slot_row == jnp.bitwise_and(own_along + 2, 3)
    slot_list = jnp.where(
        in_far,
        jnp.where(slot_list < by_ahead, slot_list, slot_list - by_ahead + FAR),
        slot_list,
    )
    row_at = lax.broadcasted_iota(jnp.int32, (8, 128), 0)
    table[...] = jnp.where(
        row_at == 0,
        in_slot,
        jnp.where(
            row_at == 1,
            home_slot,
            jnp.where(
                row_at == 2,
                in_list,
                jnp.where(
                    row_at == 3, ahead_count, jnp.where(row_at == 4, behind_count, by_ahead)
                ),
            ),
        ),
    )
    note[...] = jnp.where(
        row_at == 0,
        jnp.minimum(slot_list, 2 * FAR - 1),
        jnp.where(
            row_at == 1,
            list_slot,
            jnp.where(
                row_at == 2,
                crowded,
                jnp.where(row_at == 3, ahead_count, behind_count),
            ),
        ),
    )
    load_table = pltpu.make_async_copy(table, lookup, local_sem.at[3])
    load_table.start()

    pl.semaphore_wait(barrier, 2 * len(HOPS) + len(RAW_HOPS))
    raw_copies = {}

    def send_raw(b):
        columns = pl.ds(b * BLOCK, BLOCK)
        for i, hop in enumerate(RAW_HOPS):
            peer = raw_peer(*hop)
            raw_copies[b, i] = pltpu.make_async_remote_copy(
                src_ref=raw_ref.at[peer, 0, :, columns],
                dst_ref=gathered.at[pl.ds(aux * rows, rows), columns],
                send_sem=raw_send.at[b * len(RAW_HOPS) + i],
                recv_sem=raw_recv.at[b * len(RAW_HOPS) + i],
                device_id=(peer, orb),
                device_id_type=MESH,
            )
            raw_copies[b, i].start()

    send_raw(0)
    told, first, far, fourth, shown, passed = {}, {}, {}, {}, {}, {}

    def tell(da):
        told[da] = pltpu.make_async_remote_copy(
            src_ref=note, dst_ref=notes.at[da - 1],
            send_sem=note_send.at[da - 1], recv_sem=note_recv.at[da - 1],
            device_id=(aux, turned(da, 0)), device_id_type=MESH,
        )
        told[da].start()

    def send_first(da):
        k = da // 2
        first[da] = pltpu.make_async_remote_copy(
            src_ref=packed_out.at[k], dst_ref=mid[da],
            send_sem=p1_send.at[k], recv_sem=p1_recv.at[k],
            device_id=(aux, turned(da, 0)), device_id_type=MESH,
        )
        first[da].start()

    def send_far(da):
        k = da // 2
        first[da].wait_recv()
        start = notices[da - 1, 3 + k, 0]
        for q in range(FAR):
            packed_far[k, q] = mid[da][jnp.minimum(start + q, NEAR - 1)]
        far[da] = pltpu.make_async_remote_copy(
            src_ref=packed_far.at[k], dst_ref=mid[2].at[pl.ds(k * FAR, FAR)],
            send_sem=p1_send.at[2 + k], recv_sem=p1_recv.at[2 + k],
            device_id=(aux, turned(da, 0)), device_id_type=MESH,
        )
        far[da].start()

    def show(b):
        span = pl.ds(b * BLOCK, BLOCK)
        for k, db in enumerate((1, 3)):
            shown[b, db] = pltpu.make_async_remote_copy(
                src_ref=fitted.at[0, span], dst_ref=fitted.at[4 - db, span],
                send_sem=fit_send.at[2 * b + k], recv_sem=fit_recv.at[2 * b + k],
                device_id=(aux, turned(0, db)), device_id_type=MESH,
            )
            shown[b, db].start()

    def pass_on(b):
        for k, db in enumerate((1, 3)):
            shown[b, db].wait_recv()
            span = pl.ds(b * BLOCK + k * (BLOCK // 2), BLOCK // 2)
            passed[b, db] = pltpu.make_async_remote_copy(
                src_ref=fitted.at[4 - db, span], dst_ref=fitted.at[2, span],
                send_sem=pass_send.at[2 * b + k], recv_sem=pass_recv.at[2 * b + k],
                device_id=(aux, turned(0, db)), device_id_type=MESH,
            )
            passed[b, db].start()

    def send_fourth(da):
        at = (own_along * 16)
        for q in range(ROW):
            packed_back[da - 1, q] = back[da][notices[da - 1, 1, at + q]]
        fourth[da] = pltpu.make_async_remote_copy(
            src_ref=packed_back.at[da - 1],
            dst_ref=home.at[pl.ds(4 * CAP + (da - 1) * ROW, ROW)],
            send_sem=r2_send.at[da - 1], recv_sem=r2_recv.at[da - 1],
            device_id=(aux, turned(4 - da, 0)), device_id_type=MESH,
        )
        fourth[da].start()

    for da in HOPS:
        tell(da)
    load_coef.wait()
    load_table.wait()
    far_row = jnp.bitwise_and(own_along + 2, 3) * 16
    for da in (1, 3):
        to_row = jnp.bitwise_and(own_along + da, 3) * 16
        near_count = lookup[3 + da // 2, 0]
        skipped = lookup[5, 0] if da == 3 else 0
        for q in range(NEAR):
            beyond = jnp.clip(q - near_count + skipped, 0, 15)
            at = jnp.where(q < near_count, to_row + q, far_row + beyond)
            packed_out[da // 2, q] = coef[lookup[2, at]]
        send_first(da)
    for db in range(4):
        base = turned(0, db) * CAP
        for j in range(CAP):
            away[0, db, j] = coef[lookup[0, base + j]]
    if blocks > 1:
        send_raw(1)

    wide = pairs * npno
    of_lane = lax.broadcasted_iota(jnp.int32, (pairs, wide), 1) // npno
    in_pair = of_lane == lax.broadcasted_iota(jnp.int32, (pairs, wide), 0)
    repeat = jnp.where(
        lax.broadcasted_iota(jnp.int32, (npno, wide), 0)
        == jnp.bitwise_and(lax.broadcasted_iota(jnp.int32, (npno, wide), 1), npno - 1),
        1.0, 0.0,
    )
    choose = jnp.where(in_pair, 1.0, 0.0)
    pair_lane = lax.broadcasted_iota(jnp.int32, (1, wide), 1) // npno
    filled = jnp.zeros((1, wide), jnp.float32)
    for n in range(pairs):
        both_occupied = (
            occupied[aux * 16 + pair_orbs[0, n]] + occupied[aux * 16 + pair_orbs[1, n]]
        )
        filled = jnp.where(pair_lane == n, both_occupied, filled)
    down, along_lanes = [], []
    for k in range(2):
        level = levels[:, k, :]
        down.append(
            lax.dot_general(
                level, choose, (((0,), (0,)), ((), ())), precision=EXACT,
                preferred_element_type=jnp.float32,
            )
        )
        every = jnp.dot(level, repeat, precision=EXACT, preferred_element_type=jnp.float32)
        along_lanes.append(jnp.sum(jnp.where(in_pair, every, 0.0), axis=0, keepdims=True))
    gap[0] = down[0] + along_lanes[1] - filled
    gap[1] = down[1] + along_lanes[0] - filled

    fit_lane = lax.broadcasted_iota(jnp.int32, (16, fit), 1)
    for n in range(pairs):
        off_0 = offsets[aux * 16 + pair_orbs[0, n]]
        off_1 = offsets[aux * 16 + pair_orbs[1, n]]
        low, high = jnp.minimum(off_0, off_1), jnp.maximum(off_0, off_1)
        outside = jnp.logical_and(fit_lane >= low, fit_lane < high)
        inside[n] = jnp.where(outside, 0.0, 1.0).astype(jnp.bfloat16)

    load_inverse.wait()
    own_offset = offsets[aux * 16 + orb]
    tile = 256

    def turn(n, carry):
        start = pl.multiple_of(n * tile, tile)
        to_row = lax.broadcasted_iota(jnp.int32, (tile, fit), 0) + start
        from_row = lax.broadcasted_iota(jnp.int32, (tile, fit), 1)
        hit = jnp.bitwise_and(to_row - from_row - own_offset + 2 * fit, fit - 1) == 0
        pick = jnp.where(hit, 1.0, 0.0).astype(jnp.bfloat16)
        rolled[pl.ds(start, tile), :] = jnp.dot(
            pick, inverse[...], preferred_element_type=jnp.float32
        ).astype(jnp.bfloat16)
        return carry

    lax.fori_loop(0, fit // tile, turn, 0)

    unread = []
    for da in HOPS:
        told[da].wait_recv()
        unread.append(
            pltpu.make_async_copy(notes.at[da - 1], notices.at[da - 1], note_sem.at[da - 1])
        )
        unread[-1].start()
    flags_out[0] = jnp.maximum(
        jnp.maximum(notes[0], notes[1]), jnp.maximum(notes[2], note[...])
    )
    flag_copies = []
    for db in HOPS:
        flag_copies.append(
            pltpu.make_async_remote_copy(
                src_ref=flags_out.at[0], dst_ref=flags_across.at[db - 1],
                send_sem=across_send.at[db - 1], recv_sem=across_recv.at[db - 1],
                device_id=(aux, turned(0, db)), device_id_type=MESH,
            )
        )
        flag_copies[-1].start()
    for copy in unread:
        copy.wait()

    for copy in flag_copies:
        copy.wait()
    flags_out[1] = jnp.maximum(
        jnp.maximum(flags_across[0], flags_across[1]),
        jnp.maximum(flags_across[2], flags_out[0]),
    )
    last_flags = []
    for i, hop in enumerate(RAW_HOPS):
        last_flags.append(
            pltpu.make_async_remote_copy(
                src_ref=flags_out.at[1], dst_ref=flags_aux.at[i],
                send_sem=aux_send.at[i], recv_sem=aux_recv.at[i],
                device_id=(raw_peer(*hop), orb), device_id_type=MESH,
            )
        )
        last_flags[-1].start()

    load_own.wait()
    for b in range(blocks):
        for i in range(len(RAW_HOPS)):
            raw_copies[b, i].wait_recv()
        if b + 2 < blocks:
            send_raw(b + 2)

        def fit_tile(n, carry):
            start = pl.multiple_of(b * BLOCK + n * tile, tile)
            block = jnp.dot(
                rolled[...], gathered[:, pl.ds(start, tile)],
                preferred_element_type=jnp.float32,
            ).astype(jnp.bfloat16)
            fitted[0, pl.ds(start, tile), :] = block.T
            return carry

        lax.fori_loop(0, BLOCK // tile, fit_tile, 0)
        show(b)
        if b == FAR_AT:
            for da in (1, 3):
                send_far(da)
        if b > 0:
            pass_on(b - 1)

    for da in (1, 3, 2):
        if da == 2:
            for copy in far.values():
                copy.wait_recv()
        for db in range(4):
            base = turned(0, db) * CAP
            for j in range(CAP):
                away[da, db, j] = mid[da][notices[da - 1, 0, base + j]]

    def project(source, db, target):
        def columns(n, carry):
            start = pl.multiple_of(n * tile, tile)
            lhs = source[...].reshape(CAP * npno, dom)
            block = jnp.dot(
                lhs, fitted[db, :, pl.ds(start, tile)], preferred_element_type=jnp.float32
            ).astype(jnp.bfloat16)
            target[:, :, pl.ds(start, tile)] = block.reshape(CAP, npno, tile)
            return carry

        lax.fori_loop(0, fit // tile, columns, 0)

    def project_all(da, db):
        spots = pl.ds(db * CAP, CAP)
        project(away.at[da, db], db, home.at[spots] if da == 0 else back[da].at[spots])

    everyone = (2, 1, 3, 0)
    for da in everyone[:2]:
        project_all(da, 0)
    pass_on(blocks - 1)
    for da in everyone[2:]:
        project_all(da, 0)
    for db in (1, 3):
        for da in everyone:
            project_all(da, db)
    for copy in passed.values():
        copy.wait_recv()
    for da in everyone:
        project_all(da, 2)
        if da != 0:
            send_fourth(da)
    for da in HOPS:
        fourth[da].wait_recv()

    per = tile // npno
    lanes = 128
    packed = lanes // npno
    block_of = lax.broadcasted_iota(jnp.int32, (npno, lanes), 1) // npno
    contract = (((1,), (1,)), ((), ()))
    energies = jnp.zeros((1, lanes), jnp.float32)
    one_lane = lax.broadcasted_iota(jnp.int32, (1, lanes), 1)
    for half in range(pairs // per):
        for i in range(per):
            n = half * per + i
            one = home[lookup[1, 2 * n]]
            for part in range(npno // 16):
                left[pl.ds(i * npno + part * 16, 16), :] = (
                    one[part * 16:(part + 1) * 16] * inside[n]
                )
            right[pl.ds(i * npno, npno), :] = home[lookup[1, 2 * n + 1]]
        ahead = lax.dot_general(
            left[...], right[...], contract, preferred_element_type=jnp.float32
        )
        behind = ahead.T
        for part in range(per // packed):
            forward = jnp.zeros((npno, lanes), jnp.float32)
            swapped = jnp.zeros((npno, lanes), jnp.float32)
            for i in range(packed):
                at = (part * packed + i) * npno
                here = block_of == i
                cut = slice(part * lanes, (part + 1) * lanes)
                forward = jnp.where(here, ahead[at:at + npno, cut], forward)
                swapped = jnp.where(here, behind[at:at + npno, cut], swapped)
            first_pair = half * per + part * packed
            span = pl.ds(first_pair * npno, lanes)
            amplitude = -forward / gap[0, :, span]
            mirrored = -swapped / gap[1, :, span]
            share = jnp.sum(
                forward * (2.0 * amplitude - mirrored), axis=0, keepdims=True
            )
            for shift in (1, 2, 4, 8, 16):
                share = share + pltpu.roll(share, lanes - shift, 1)
            for i in range(packed):
                n = first_pair + i
                energies = jnp.where(
                    one_lane == n, pltpu.roll(share, (n - i * npno) % lanes, 1), energies
                )
            spread[...] = amplitude
            strided = [spread[pl.ds(u, npno // packed, stride=packed), :] for u in range(packed)]
            for i in range(packed):
                line = jnp.zeros((npno // packed, lanes), jnp.float32)
                for u in range(packed):
                    moved = pltpu.roll(strided[u], ((u - i) * npno) % lanes, 1)
                    line = jnp.where(block_of[:npno // packed] == u, moved, line)
                n = first_pair + i
                for t in range(npno // packed):
                    out_ref[n:n + 1, t * lanes:(t + 1) * lanes] = line[t:t + 1]
    energy_ref[...] = energies
    every_flag = flags_out[1]
    for i, copy in enumerate(last_flags):
        copy.wait()
        every_flag = jnp.maximum(every_flag, flags_aux[i])
    crowded_ref[0] = jnp.max(every_flag[2:3])

    for group in (raw_copies, told, first, far, shown, passed, fourth):
        for copy in group.values():
            copy.wait_send()


def align_rows(shifted_in, begin_at):
    return lax.dynamic_slice_in_dim(shifted_in, begin_at, shifted_in.shape[1] * 2 // 3, 1)


def spread_out(raw_ints, fit_inverse, pair_orbs, pno_coef, pno_energy, occ_energy, fit_offset):
    orb_count = lax.axis_size("orb")
    region = lax.axis_index("aux")
    inverse = fit_inverse[0]
    gathered = lax.all_to_all(raw_ints, "aux", split_axis=0, concat_axis=2, tiled=True)
    fitted = jnp.dot(inverse, gathered[0, 0], preferred_element_type=jnp.float32).astype(
        jnp.bfloat16
    )
    fit_rows = fitted.shape[0]
    pair_count = pair_orbs.shape[0]
    pno_count = pno_coef.shape[2]
    dom_count = pno_coef.shape[3]
    side_count = 2 * pair_count
    capacity = max(2, 4 * pair_count // orb_count)
    slot_count = orb_count * capacity
    side_orbs = pair_orbs.reshape(side_count)
    matches = side_orbs[:, None] == side_orbs[None, :]
    sequence = jnp.arange(side_count, dtype=jnp.int32)
    earlier = sequence[None, :] < sequence[:, None]
    position = jnp.sum(jnp.where(matches & earlier, 1, 0), axis=1)
    slot_index = side_orbs * capacity + position
    placing = jnp.where(
        slot_index[None, :] == jnp.arange(slot_count, dtype=jnp.int32)[:, None], 1.0, 0.0
    ).astype(jnp.bfloat16)
    outgoing = jnp.dot(
        placing,
        pno_coef.reshape(side_count, pno_count * dom_count),
        preferred_element_type=jnp.float32,
    ).astype(jnp.bfloat16)
    outgoing = outgoing.reshape(orb_count, capacity, pno_count, dom_count)
    projected = jnp.einsum(
        "scpd,fd->scpf",
        lax.all_to_all(outgoing, "orb", split_axis=0, concat_axis=0, tiled=True),
        fitted,
        preferred_element_type=jnp.float32,
    ).astype(jnp.bfloat16)
    returned = lax.all_to_all(projected, "orb", split_axis=0, concat_axis=0, tiled=True)
    side_blocks = jnp.dot(
        placing.T,
        returned.reshape(slot_count, pno_count * fit_rows),
        preferred_element_type=jnp.float32,
    ).astype(jnp.bfloat16)
    side_blocks = side_blocks.reshape(pair_count, 2, pno_count, fit_rows)
    orb_total = occ_energy.shape[0]
    global_orb = region * orb_count + pair_orbs
    selector = global_orb[:, :, None] == jnp.arange(orb_total, dtype=jnp.int32)[None, None, :]
    offsets = jnp.sum(jnp.where(selector, fit_offset[None, None, :], 0), axis=2)
    occupied = jnp.sum(jnp.where(selector, occ_energy[None, None, :], 0.0), axis=2)
    margin = fit_rows // 4
    shift_rows = offsets[:, 0] - offsets[:, 1]
    padded = jnp.pad(side_blocks[:, 1], ((0, 0), (0, 0), (margin, margin)))
    aligned = jax.vmap(align_rows)(padded, margin + shift_rows)
    coupling = jnp.einsum(
        "npr,nqr->npq", side_blocks[:, 0], aligned, preferred_element_type=jnp.float32
    )
    denominator = (
        pno_energy[:, 0, :, None]
        + pno_energy[:, 1, None, :]
        - occupied[:, 0, None, None]
        - occupied[:, 1, None, None]
    )
    amplitude = -coupling / denominator
    energy = jnp.sum(coupling * (2.0 * amplitude - jnp.swapaxes(amplitude, 1, 2)), axis=(1, 2))
    return (amplitude.reshape(pair_count, pno_count * pno_count), energy)


def on_device(raw_ints, fit_inverse, pair_orbs, pno_coef, pno_energy, occ_energy, fit_offset):
    pairs, _, npno, dom = pno_coef.shape
    fit = fit_inverse.shape[1]
    bf16 = jnp.bfloat16
    f32 = jnp.float32
    i32 = jnp.int32
    blocks = dom // BLOCK
    vmem = pltpu.VMEM
    dma = pltpu.SemaphoreType.DMA
    smem_spec = pl.BlockSpec(memory_space=pltpu.SMEM)
    vmem_spec = pl.BlockSpec(memory_space=pltpu.VMEM)
    any_spec = pl.BlockSpec(memory_space=pl.ANY)
    amplitude, energy, crowded = pl.pallas_call(
        exchange_kernel,
        out_shape=(
            jax.ShapeDtypeStruct((pairs, npno * npno), f32),
            jax.ShapeDtypeStruct((1, 128), f32),
            jax.ShapeDtypeStruct((1,), i32),
        ),
        in_specs=[smem_spec] * 3 + [vmem_spec] + [any_spec] * 3,
        out_specs=(vmem_spec, vmem_spec, smem_spec),
        scratch_shapes=[
            vmem((2 * pairs, npno, dom), bf16),
            vmem((fit, fit), bf16),
            vmem((fit, fit), bf16),
            vmem((fit, dom), bf16),
            vmem((4, dom, fit), bf16),
            vmem((2, NEAR, npno, dom), bf16),
            vmem((2, FAR, npno, dom), bf16),
            vmem((NEAR, npno, dom), bf16),
            vmem((2 * FAR, npno, dom), bf16),
            vmem((NEAR, npno, dom), bf16),
            vmem((4, 4, CAP, npno, dom), bf16),
            vmem((4 * CAP, npno, fit), bf16),
            vmem((4 * CAP, npno, fit), bf16),
            vmem((4 * CAP, npno, fit), bf16),
            vmem((3, ROW, npno, fit), bf16),
            vmem((4 * CAP + 3 * ROW, npno, fit), bf16),
            vmem((256, fit), bf16),
            vmem((256, fit), bf16),
            vmem((pairs, 16, fit), bf16),
            vmem((2, npno, pairs * npno), f32),
            vmem((npno, 128), f32),
            vmem((8, 128), i32),
            vmem((8, 128), i32),
            vmem((3, 8, 128), i32),
            vmem((2, 8, 128), i32),
            vmem((3, 8, 128), i32),
            vmem((7, 8, 128), i32),
            pltpu.SMEM((8, 128), i32),
            pltpu.SMEM((3, 8, 128), i32),
            dma((4,)), dma((7 * blocks,)), dma((7 * blocks,)),
            dma((4,)), dma((4,)), dma((2 * blocks,)), dma((2 * blocks,)),
            dma((2 * blocks,)), dma((2 * blocks,)), dma((3,)), dma((3,)),
            dma((3,)), dma((3,)), dma((3,)),
            dma((3,)), dma((3,)), dma((7,)), dma((7,)),
        ],
        compiler_params=pltpu.CompilerParams(
            collective_id=0, has_side_effects=True, vmem_limit_bytes=58 * 2**20
        ),
        name="exchange",
    )(
        pair_orbs.T, fit_offset, occ_energy, pno_energy,
        raw_ints, fit_inverse, pno_coef.reshape(2 * pairs, npno, dom),
    )
    return lax.cond(
        crowded[0] > 0,
        lambda: spread_out(
            raw_ints, fit_inverse, pair_orbs, pno_coef, pno_energy, occ_energy, fit_offset
        ),
        lambda: (amplitude, energy[0, :pairs]),
    )


def solution(mesh):
    return jax.shard_map(
        on_device,
        mesh=mesh,
        in_specs=(
            P(None, "orb", "aux", None),
            P(("aux", "orb"), None, None),
            P(("aux", "orb"), None),
            P(("aux", "orb"), None, None, None),
            P(("aux", "orb"), None, None),
            P(),
            P(),
        ),
        out_specs=(P(("aux", "orb"), None), P(("aux", "orb"))),
        check_vma=False,
    )
```

```python
import jax
import jax.numpy as jnp
from jax import lax
from jax.experimental import pallas as pl
from jax.experimental.pallas import tpu as pltpu
from jax.sharding import PartitionSpec as P

MESH = pl.DeviceIdType.MESH
HOPS = (1, 3, 2)
RAW_HOPS = ((0, 1), (1, 0), (3, 0), (1, 1), (3, 1), (2, 0), (2, 1))
CAP = 4
ROW = 11
NEAR = 14
FAR = 6
FAR_AT = 1
BLOCK = 512
EXACT = lax.Precision.HIGHEST


def exchange_kernel(
    pair_orbs, offsets, occupied, levels, raw_ref, inv_ref, coef_ref,
    out_ref, energy_ref, crowded_ref,
    coef, inverse, rolled, gathered, fitted, packed_out, packed_far, mid_1, mid_2, mid_3, away,
    back_1, back_2, back_3, packed_back, home,
    left, right, inside, gap, spread, table, note, notes, flags_out, flags_across, flags_aux,
    lookup, notices,
    local_sem, raw_send, raw_recv, p1_send, p1_recv, fit_send, fit_recv,
    pass_send, pass_recv, r2_send, r2_recv, note_send, note_recv, note_sem,
    across_send, across_recv, aux_send, aux_recv,
):
    mid = {1: mid_1, 2: mid_2, 3: mid_3}
    back = {1: back_1, 2: back_2, 3: back_3}
    aux = lax.axis_index("aux")
    orb = lax.axis_index("orb")
    x, core = aux // 2, lax.rem(aux, 2)
    y, z = orb // 4, lax.rem(orb, 4)
    fit = inverse.shape[0]
    dom = fitted.shape[1]
    blocks = dom // BLOCK
    side_count, npno, _ = coef.shape
    pairs = side_count // 2
    rows = raw_ref.shape[2]

    def turned(d_first, d_second):
        dy = jnp.where(core == 0, d_first, d_second)
        dz = jnp.where(core == 0, d_second, d_first)
        return lax.rem(y + dy, 4) * 4 + lax.rem(z + dz, 4)

    def raw_peer(dx, dc):
        return lax.rem(x + dx, 4) * 2 + lax.rem(core + dc, 2)

    load_coef = pltpu.make_async_copy(coef_ref, coef, local_sem.at[0])
    load_inverse = pltpu.make_async_copy(inv_ref.at[0], inverse, local_sem.at[1])
    load_own = pltpu.make_async_copy(
        raw_ref.at[aux, 0], gathered.at[pl.ds(aux * rows, rows)], local_sem.at[2]
    )
    load_coef.start()
    load_inverse.start()
    load_own.start()

    barrier = pltpu.get_barrier_semaphore()
    for d in HOPS:
        pl.semaphore_signal(barrier, 1, device_id=(aux, turned(d, 0)), device_id_type=MESH)
        pl.semaphore_signal(barrier, 1, device_id=(aux, turned(0, d)), device_id_type=MESH)
    for hop in RAW_HOPS:
        pl.semaphore_signal(barrier, 1, device_id=(raw_peer(*hop), orb), device_id_type=MESH)

    own_along = jnp.where(core == 0, y, z)
    own_across = jnp.where(core == 0, z, y)

    def row_of(p):
        return jnp.where(core == 0, p // 4, jnp.bitwise_and(p, 3))

    def place_in_row(p):
        return jnp.where(core == 0, jnp.bitwise_and(p, 3), p // 4)

    lane = lax.broadcasted_iota(jnp.int32, (8, 128), 1)
    slot_orb, slot_place = lane // CAP, jnp.bitwise_and(lane, CAP - 1)
    slot_row = row_of(slot_orb)
    list_row, list_place = lane // 16, jnp.bitwise_and(lane, 15)
    zero = jnp.zeros((8, 128), jnp.int32)
    in_slot, in_list, list_orb, slot_list = zero, zero, zero, zero
    seen, seen_row, seen_list, own_orb = zero, zero, zero, zero
    for i in range(side_count):
        name = pair_orbs[i % 2, i // 2]
        row = row_of(name)
        match = slot_orb == name
        hit = jnp.logical_and(match, seen == slot_place)
        in_slot = jnp.where(hit, i, in_slot)
        slot_list = jnp.where(hit, seen_row, slot_list)
        seen = seen + jnp.where(match, 1, 0)
        seen_row = seen_row + jnp.where(slot_row == row, 1, 0)
        match = list_row == row
        hit = jnp.logical_and(match, seen_list == list_place)
        in_list = jnp.where(hit, i, in_list)
        list_orb = jnp.where(hit, name, list_orb)
        seen_list = seen_list + jnp.where(match, 1, 0)
        own_orb = jnp.where(lane == i, name, own_orb)
    own_row = row_of(own_orb)
    side_place, side_list, list_spot = zero, zero, zero
    for i in range(side_count):
        name = pair_orbs[i % 2, i // 2]
        after = lane > i
        side_place = side_place + jnp.where(jnp.logical_and(own_orb == name, after), 1, 0)
        side_list = side_list + jnp.where(
            jnp.logical_and(own_row == row_of(name), after), 1, 0
        )
        list_spot = list_spot + jnp.where(
            jnp.logical_and(list_orb == name, in_list > i), 1, 0
        )
    along = jnp.bitwise_and(own_row + 4 - own_along, 3)
    across = jnp.bitwise_and(place_in_row(own_orb) + 4 - own_across, 3)
    home_slot = jnp.where(
        along == 0,
        across * CAP + jnp.minimum(side_place, CAP - 1),
        4 * CAP + (along - 1) * ROW + jnp.minimum(side_list, ROW - 1),
    )
    list_slot = (
        jnp.bitwise_and(place_in_row(list_orb) + 4 - own_across, 3) * CAP
        + jnp.minimum(list_spot, CAP - 1)
    )
    def named(step):
        there = list_row == jnp.bitwise_and(own_along + step, 3)
        return jnp.max(jnp.where(there, seen_list, 0))

    ahead_count, far_count, behind_count = named(1), named(2), named(3)
    by_ahead = jnp.minimum(jnp.minimum(far_count, FAR), jnp.maximum(NEAR - ahead_count, 0))
    by_behind = far_count - by_ahead
    fits = jnp.logical_and(
        jnp.logical_and(ahead_count <= ROW, behind_count <= ROW),
        jnp.logical_and(
            far_count <= ROW,
            jnp.logical_and(by_behind <= FAR, behind_count + by_behind <= NEAR),
        ),
    )
    crowded = jnp.where(fits, 0, 1)
    in_far = slot_row == jnp.bitwise_and(own_along + 2, 3)
    slot_list = jnp.where(
        in_far,
        jnp.where(slot_list < by_ahead, slot_list, slot_list - by_ahead + FAR),
        slot_list,
    )
    row_at = lax.broadcasted_iota(jnp.int32, (8, 128), 0)
    table[...] = jnp.where(
        row_at == 0,
        in_slot,
        jnp.where(
            row_at == 1,
            home_slot,
            jnp.where(
                row_at == 2,
                in_list,
                jnp.where(
                    row_at == 3, ahead_count, jnp.where(row_at == 4, behind_count, by_ahead)
                ),
            ),
        ),
    )
    note[...] = jnp.where(
        row_at == 0,
        jnp.minimum(slot_list, 2 * FAR - 1),
        jnp.where(
            row_at == 1,
            list_slot,
            jnp.where(
                row_at == 2,
                crowded,
                jnp.where(row_at == 3, ahead_count, behind_count),
            ),
        ),
    )
    load_table = pltpu.make_async_copy(table, lookup, local_sem.at[3])
    load_table.start()

    pl.semaphore_wait(barrier, 2 * len(HOPS) + len(RAW_HOPS))
    raw_copies = {}

    def send_raw(b):
        columns = pl.ds(b * BLOCK, BLOCK)
        for i, hop in enumerate(RAW_HOPS):
            peer = raw_peer(*hop)
            raw_copies[b, i] = pltpu.make_async_remote_copy(
                src_ref=raw_ref.at[peer, 0, :, columns],
                dst_ref=gathered.at[pl.ds(aux * rows, rows), columns],
                send_sem=raw_send.at[b * len(RAW_HOPS) + i],
                recv_sem=raw_recv.at[b * len(RAW_HOPS) + i],
                device_id=(peer, orb),
                device_id_type=MESH,
            )
            raw_copies[b, i].start()

    send_raw(0)
    told, first, far, fourth, shown, passed = {}, {}, {}, {}, {}, {}

    def tell(da):
        told[da] = pltpu.make_async_remote_copy(
            src_ref=note, dst_ref=notes.at[da - 1],
            send_sem=note_send.at[da - 1], recv_sem=note_recv.at[da - 1],
            device_id=(aux, turned(da, 0)), device_id_type=MESH,
        )
        told[da].start()

    def send_first(da):
        k = da // 2
        first[da] = pltpu.make_async_remote_copy(
            src_ref=packed_out.at[k], dst_ref=mid[da],
            send_sem=p1_send.at[k], recv_sem=p1_recv.at[k],
            device_id=(aux, turned(da, 0)), device_id_type=MESH,
        )
        first[da].start()

    def send_far(da):
        k = da // 2
        first[da].wait_recv()
        start = notices[da - 1, 3 + k, 0]
        for q in range(FAR):
            packed_far[k, q] = mid[da][jnp.minimum(start + q, NEAR - 1)]
        far[da] = pltpu.make_async_remote_copy(
            src_ref=packed_far.at[k], dst_ref=mid[2].at[pl.ds(k * FAR, FAR)],
            send_sem=p1_send.at[2 + k], recv_sem=p1_recv.at[2 + k],
            device_id=(aux, turned(da, 0)), device_id_type=MESH,
        )
        far[da].start()

    def show(b):
        span = pl.ds(b * BLOCK, BLOCK)
        for k, db in enumerate((1, 3)):
            shown[b, db] = pltpu.make_async_remote_copy(
                src_ref=fitted.at[0, span], dst_ref=fitted.at[4 - db, span],
                send_sem=fit_send.at[2 * b + k], recv_sem=fit_recv.at[2 * b + k],
                device_id=(aux, turned(0, db)), device_id_type=MESH,
            )
            shown[b, db].start()

    def pass_on(b):
        for k, db in enumerate((1, 3)):
            shown[b, db].wait_recv()
            span = pl.ds(b * BLOCK + k * (BLOCK // 2), BLOCK // 2)
            passed[b, db] = pltpu.make_async_remote_copy(
                src_ref=fitted.at[4 - db, span], dst_ref=fitted.at[2, span],
                send_sem=pass_send.at[2 * b + k], recv_sem=pass_recv.at[2 * b + k],
                device_id=(aux, turned(0, db)), device_id_type=MESH,
            )
            passed[b, db].start()

    def send_fourth(da):
        at = (own_along * 16)
        for q in range(ROW):
            packed_back[da - 1, q] = back[da][notices[da - 1, 1, at + q]]
        fourth[da] = pltpu.make_async_remote_copy(
            src_ref=packed_back.at[da - 1],
            dst_ref=home.at[pl.ds(4 * CAP + (da - 1) * ROW, ROW)],
            send_sem=r2_send.at[da - 1], recv_sem=r2_recv.at[da - 1],
            device_id=(aux, turned(4 - da, 0)), device_id_type=MESH,
        )
        fourth[da].start()

    for da in HOPS:
        tell(da)
    load_coef.wait()
    load_table.wait()
    far_row = jnp.bitwise_and(own_along + 2, 3) * 16
    for da in (1, 3):
        to_row = jnp.bitwise_and(own_along + da, 3) * 16
        near_count = lookup[3 + da // 2, 0]
        skipped = lookup[5, 0] if da == 3 else 0
        for q in range(NEAR):
            beyond = jnp.clip(q - near_count + skipped, 0, 15)
            at = jnp.where(q < near_count, to_row + q, far_row + beyond)
            packed_out[da // 2, q] = coef[lookup[2, at]]
        send_first(da)
    for db in range(4):
        base = turned(0, db) * CAP
        for j in range(CAP):
            away[db, 0, j] = coef[lookup[0, base + j]]
    if blocks > 1:
        send_raw(1)

    wide = pairs * npno
    of_lane = lax.broadcasted_iota(jnp.int32, (pairs, wide), 1) // npno
    in_pair = of_lane == lax.broadcasted_iota(jnp.int32, (pairs, wide), 0)
    repeat = jnp.where(
        lax.broadcasted_iota(jnp.int32, (npno, wide), 0)
        == jnp.bitwise_and(lax.broadcasted_iota(jnp.int32, (npno, wide), 1), npno - 1),
        1.0, 0.0,
    )
    choose = jnp.where(in_pair, 1.0, 0.0)
    pair_lane = lax.broadcasted_iota(jnp.int32, (1, wide), 1) // npno
    filled = jnp.zeros((1, wide), jnp.float32)
    for n in range(pairs):
        both_occupied = (
            occupied[aux * 16 + pair_orbs[0, n]] + occupied[aux * 16 + pair_orbs[1, n]]
        )
        filled = jnp.where(pair_lane == n, both_occupied, filled)
    down, along_lanes = [], []
    for k in range(2):
        level = levels[:, k, :]
        down.append(
            lax.dot_general(
                level, choose, (((0,), (0,)), ((), ())), precision=EXACT,
                preferred_element_type=jnp.float32,
            )
        )
        every = jnp.dot(level, repeat, precision=EXACT, preferred_element_type=jnp.float32)
        along_lanes.append(jnp.sum(jnp.where(in_pair, every, 0.0), axis=0, keepdims=True))
    gap[0] = down[0] + along_lanes[1] - filled
    gap[1] = down[1] + along_lanes[0] - filled

    fit_lane = lax.broadcasted_iota(jnp.int32, (16, fit), 1)
    for n in range(pairs):
        off_0 = offsets[aux * 16 + pair_orbs[0, n]]
        off_1 = offsets[aux * 16 + pair_orbs[1, n]]
        low, high = jnp.minimum(off_0, off_1), jnp.maximum(off_0, off_1)
        outside = jnp.logical_and(fit_lane >= low, fit_lane < high)
        inside[n] = jnp.where(outside, 0.0, 1.0).astype(jnp.bfloat16)

    load_inverse.wait()
    own_offset = offsets[aux * 16 + orb]
    tile = 256

    def turn(n, carry):
        start = pl.multiple_of(n * tile, tile)
        to_row = lax.broadcasted_iota(jnp.int32, (tile, fit), 0) + start
        from_row = lax.broadcasted_iota(jnp.int32, (tile, fit), 1)
        hit = jnp.bitwise_and(to_row - from_row - own_offset + 2 * fit, fit - 1) == 0
        pick = jnp.where(hit, 1.0, 0.0).astype(jnp.bfloat16)
        rolled[pl.ds(start, tile), :] = jnp.dot(
            pick, inverse[...], preferred_element_type=jnp.float32
        ).astype(jnp.bfloat16)
        return carry

    lax.fori_loop(0, fit // tile, turn, 0)

    unread = []
    for da in HOPS:
        told[da].wait_recv()
        unread.append(
            pltpu.make_async_copy(notes.at[da - 1], notices.at[da - 1], note_sem.at[da - 1])
        )
        unread[-1].start()
    flags_out[0] = jnp.maximum(
        jnp.maximum(notes[0], notes[1]), jnp.maximum(notes[2], note[...])
    )
    flag_copies = []
    for db in HOPS:
        flag_copies.append(
            pltpu.make_async_remote_copy(
                src_ref=flags_out.at[0], dst_ref=flags_across.at[db - 1],
                send_sem=across_send.at[db - 1], recv_sem=across_recv.at[db - 1],
                device_id=(aux, turned(0, db)), device_id_type=MESH,
            )
        )
        flag_copies[-1].start()
    for copy in unread:
        copy.wait()

    for copy in flag_copies:
        copy.wait()
    flags_out[1] = jnp.maximum(
        jnp.maximum(flags_across[0], flags_across[1]),
        jnp.maximum(flags_across[2], flags_out[0]),
    )
    last_flags = []
    for i, hop in enumerate(RAW_HOPS):
        last_flags.append(
            pltpu.make_async_remote_copy(
                src_ref=flags_out.at[1], dst_ref=flags_aux.at[i],
                send_sem=aux_send.at[i], recv_sem=aux_recv.at[i],
                device_id=(raw_peer(*hop), orb), device_id_type=MESH,
            )
        )
        last_flags[-1].start()

    load_own.wait()
    for b in range(blocks):
        for i in range(len(RAW_HOPS)):
            raw_copies[b, i].wait_recv()
        if b + 2 < blocks:
            send_raw(b + 2)

        def fit_tile(n, carry):
            start = pl.multiple_of(b * BLOCK + n * tile, tile)
            block = jnp.dot(
                rolled[...], gathered[:, pl.ds(start, tile)],
                preferred_element_type=jnp.float32,
            ).astype(jnp.bfloat16)
            fitted[0, pl.ds(start, tile), :] = block.T
            return carry

        lax.fori_loop(0, BLOCK // tile, fit_tile, 0)
        show(b)
        if b == FAR_AT:
            for da in (1, 3):
                send_far(da)
        if b > 0:
            pass_on(b - 1)

    for da in (1, 3, 2):
        if da == 2:
            for copy in far.values():
                copy.wait_recv()
        for db in range(4):
            base = turned(0, db) * CAP
            for j in range(CAP):
                away[db, da, j] = mid[da][notices[da - 1, 0, base + j]]

    def project(source, db, target):
        def columns(n, carry):
            start = pl.multiple_of(n * tile, tile)
            lhs = source[...].reshape(CAP * npno, dom)
            block = jnp.dot(
                lhs, fitted[db, :, pl.ds(start, tile)], preferred_element_type=jnp.float32
            ).astype(jnp.bfloat16)
            target[:, :, pl.ds(start, tile)] = block.reshape(CAP, npno, tile)
            return carry

        lax.fori_loop(0, fit // tile, columns, 0)

    def project_all(da, db):
        spots = pl.ds(db * CAP, CAP)
        project(away.at[db, da], db, home.at[spots] if da == 0 else back[da].at[spots])

    everyone = (2, 1, 3, 0)

    def project_group(db):
        spots = pl.ds(db * CAP, CAP)

        def columns(n, carry):
            span = pl.ds(pl.multiple_of(n * tile, tile), tile)
            block = jnp.dot(
                away[db].reshape(4 * CAP * npno, dom), fitted[db, :, span],
                preferred_element_type=jnp.float32,
            ).astype(jnp.bfloat16).reshape(4, CAP, npno, tile)
            home[spots, :, span] = block[0]
            for da in HOPS:
                back[da][spots, :, span] = block[da]
            return carry

        lax.fori_loop(0, fit // tile, columns, 0)

    project_group(0)
    pass_on(blocks - 1)
    project_group(1)
    project_group(3)
    for copy in passed.values():
        copy.wait_recv()
    for da in everyone:
        project_all(da, 2)
        if da != 0:
            send_fourth(da)
    for da in HOPS:
        fourth[da].wait_recv()

    per = tile // npno
    lanes = 128
    packed = lanes // npno
    block_of = lax.broadcasted_iota(jnp.int32, (npno, lanes), 1) // npno
    contract = (((1,), (1,)), ((), ()))
    energies = jnp.zeros((1, lanes), jnp.float32)
    one_lane = lax.broadcasted_iota(jnp.int32, (1, lanes), 1)
    for half in range(pairs // per):
        for i in range(per):
            n = half * per + i
            one = home[lookup[1, 2 * n]]
            for part in range(npno // 16):
                left[pl.ds(i * npno + part * 16, 16), :] = (
                    one[part * 16:(part + 1) * 16] * inside[n]
                )
            right[pl.ds(i * npno, npno), :] = home[lookup[1, 2 * n + 1]]
        ahead = lax.dot_general(
            left[...], right[...], contract, preferred_element_type=jnp.float32
        )
        behind = ahead.T
        for part in range(per // packed):
            forward = jnp.zeros((npno, lanes), jnp.float32)
            swapped = jnp.zeros((npno, lanes), jnp.float32)
            for i in range(packed):
                at = (part * packed + i) * npno
                here = block_of == i
                cut = slice(part * lanes, (part + 1) * lanes)
                forward = jnp.where(here, ahead[at:at + npno, cut], forward)
                swapped = jnp.where(here, behind[at:at + npno, cut], swapped)
            first_pair = half * per + part * packed
            span = pl.ds(first_pair * npno, lanes)
            amplitude = -forward / gap[0, :, span]
            mirrored = -swapped / gap[1, :, span]
            share = jnp.sum(
                forward * (2.0 * amplitude - mirrored), axis=0, keepdims=True
            )
            for shift in (1, 2, 4, 8, 16):
                share = share + pltpu.roll(share, lanes - shift, 1)
            for i in range(packed):
                n = first_pair + i
                energies = jnp.where(
                    one_lane == n, pltpu.roll(share, (n - i * npno) % lanes, 1), energies
                )
            spread[...] = amplitude
            strided = [spread[pl.ds(u, npno // packed, stride=packed), :] for u in range(packed)]
            for i in range(packed):
                line = jnp.zeros((npno // packed, lanes), jnp.float32)
                for u in range(packed):
                    moved = pltpu.roll(strided[u], ((u - i) * npno) % lanes, 1)
                    line = jnp.where(block_of[:npno // packed] == u, moved, line)
                n = first_pair + i
                for t in range(npno // packed):
                    out_ref[n:n + 1, t * lanes:(t + 1) * lanes] = line[t:t + 1]
    energy_ref[...] = energies
    every_flag = flags_out[1]
    for i, copy in enumerate(last_flags):
        copy.wait()
        every_flag = jnp.maximum(every_flag, flags_aux[i])
    crowded_ref[0] = jnp.max(every_flag[2:3])

    for group in (raw_copies, told, first, far, shown, passed, fourth):
        for copy in group.values():
            copy.wait_send()


def align_rows(shifted_in, begin_at):
    return lax.dynamic_slice_in_dim(shifted_in, begin_at, shifted_in.shape[1] * 2 // 3, 1)


def spread_out(raw_ints, fit_inverse, pair_orbs, pno_coef, pno_energy, occ_energy, fit_offset):
    orb_count = lax.axis_size("orb")
    region = lax.axis_index("aux")
    inverse = fit_inverse[0]
    gathered = lax.all_to_all(raw_ints, "aux", split_axis=0, concat_axis=2, tiled=True)
    fitted = jnp.dot(inverse, gathered[0, 0], preferred_element_type=jnp.float32).astype(
        jnp.bfloat16
    )
    fit_rows = fitted.shape[0]
    pair_count = pair_orbs.shape[0]
    pno_count = pno_coef.shape[2]
    dom_count = pno_coef.shape[3]
    side_count = 2 * pair_count
    capacity = max(2, 4 * pair_count // orb_count)
    slot_count = orb_count * capacity
    side_orbs = pair_orbs.reshape(side_count)
    matches = side_orbs[:, None] == side_orbs[None, :]
    sequence = jnp.arange(side_count, dtype=jnp.int32)
    earlier = sequence[None, :] < sequence[:, None]
    position = jnp.sum(jnp.where(matches & earlier, 1, 0), axis=1)
    slot_index = side_orbs * capacity + position
    placing = jnp.where(
        slot_index[None, :] == jnp.arange(slot_count, dtype=jnp.int32)[:, None], 1.0, 0.0
    ).astype(jnp.bfloat16)
    outgoing = jnp.dot(
        placing,
        pno_coef.reshape(side_count, pno_count * dom_count),
        preferred_element_type=jnp.float32,
    ).astype(jnp.bfloat16)
    outgoing = outgoing.reshape(orb_count, capacity, pno_count, dom_count)
    projected = jnp.einsum(
        "scpd,fd->scpf",
        lax.all_to_all(outgoing, "orb", split_axis=0, concat_axis=0, tiled=True),
        fitted,
        preferred_element_type=jnp.float32,
    ).astype(jnp.bfloat16)
    returned = lax.all_to_all(projected, "orb", split_axis=0, concat_axis=0, tiled=True)
    side_blocks = jnp.dot(
        placing.T,
        returned.reshape(slot_count, pno_count * fit_rows),
        preferred_element_type=jnp.float32,
    ).astype(jnp.bfloat16)
    side_blocks = side_blocks.reshape(pair_count, 2, pno_count, fit_rows)
    orb_total = occ_energy.shape[0]
    global_orb = region * orb_count + pair_orbs
    selector = global_orb[:, :, None] == jnp.arange(orb_total, dtype=jnp.int32)[None, None, :]
    offsets = jnp.sum(jnp.where(selector, fit_offset[None, None, :], 0), axis=2)
    occupied = jnp.sum(jnp.where(selector, occ_energy[None, None, :], 0.0), axis=2)
    margin = fit_rows // 4
    shift_rows = offsets[:, 0] - offsets[:, 1]
    padded = jnp.pad(side_blocks[:, 1], ((0, 0), (0, 0), (margin, margin)))
    aligned = jax.vmap(align_rows)(padded, margin + shift_rows)
    coupling = jnp.einsum(
        "npr,nqr->npq", side_blocks[:, 0], aligned, preferred_element_type=jnp.float32
    )
    denominator = (
        pno_energy[:, 0, :, None]
        + pno_energy[:, 1, None, :]
        - occupied[:, 0, None, None]
        - occupied[:, 1, None, None]
    )
    amplitude = -coupling / denominator
    energy = jnp.sum(coupling * (2.0 * amplitude - jnp.swapaxes(amplitude, 1, 2)), axis=(1, 2))
    return (amplitude.reshape(pair_count, pno_count * pno_count), energy)


def on_device(raw_ints, fit_inverse, pair_orbs, pno_coef, pno_energy, occ_energy, fit_offset):
    pairs, _, npno, dom = pno_coef.shape
    fit = fit_inverse.shape[1]
    bf16 = jnp.bfloat16
    f32 = jnp.float32
    i32 = jnp.int32
    blocks = dom // BLOCK
    vmem = pltpu.VMEM
    dma = pltpu.SemaphoreType.DMA
    smem_spec = pl.BlockSpec(memory_space=pltpu.SMEM)
    vmem_spec = pl.BlockSpec(memory_space=pltpu.VMEM)
    any_spec = pl.BlockSpec(memory_space=pl.ANY)
    amplitude, energy, crowded = pl.pallas_call(
        exchange_kernel,
        out_shape=(
            jax.ShapeDtypeStruct((pairs, npno * npno), f32),
            jax.ShapeDtypeStruct((1, 128), f32),
            jax.ShapeDtypeStruct((1,), i32),
        ),
        in_specs=[smem_spec] * 3 + [vmem_spec] + [any_spec] * 3,
        out_specs=(vmem_spec, vmem_spec, smem_spec),
        scratch_shapes=[
            vmem((2 * pairs, npno, dom), bf16),
            vmem((fit, fit), bf16),
            vmem((fit, fit), bf16),
            vmem((fit, dom), bf16),
            vmem((4, dom, fit), bf16),
            vmem((2, NEAR, npno, dom), bf16),
            vmem((2, FAR, npno, dom), bf16),
            vmem((NEAR, npno, dom), bf16),
            vmem((2 * FAR, npno, dom), bf16),
            vmem((NEAR, npno, dom), bf16),
            vmem((4, 4, CAP, npno, dom), bf16),
            vmem((4 * CAP, npno, fit), bf16),
            vmem((4 * CAP, npno, fit), bf16),
            vmem((4 * CAP, npno, fit), bf16),
            vmem((3, ROW, npno, fit), bf16),
            vmem((4 * CAP + 3 * ROW, npno, fit), bf16),
            vmem((256, fit), bf16),
            vmem((256, fit), bf16),
            vmem((pairs, 16, fit), bf16),
            vmem((2, npno, pairs * npno), f32),
            vmem((npno, 128), f32),
            vmem((8, 128), i32),
            vmem((8, 128), i32),
            vmem((3, 8, 128), i32),
            vmem((2, 8, 128), i32),
            vmem((3, 8, 128), i32),
            vmem((7, 8, 128), i32),
            pltpu.SMEM((8, 128), i32),
            pltpu.SMEM((3, 8, 128), i32),
            dma((4,)), dma((7 * blocks,)), dma((7 * blocks,)),
            dma((4,)), dma((4,)), dma((2 * blocks,)), dma((2 * blocks,)),
            dma((2 * blocks,)), dma((2 * blocks,)), dma((3,)), dma((3,)),
            dma((3,)), dma((3,)), dma((3,)),
            dma((3,)), dma((3,)), dma((7,)), dma((7,)),
        ],
        compiler_params=pltpu.CompilerParams(
            collective_id=0, has_side_effects=True, vmem_limit_bytes=58 * 2**20
        ),
        name="exchange",
    )(
        pair_orbs.T, fit_offset, occ_energy, pno_energy,
        raw_ints, fit_inverse, pno_coef.reshape(2 * pairs, npno, dom),
    )
    return lax.cond(
        crowded[0] > 0,
        lambda: spread_out(
            raw_ints, fit_inverse, pair_orbs, pno_coef, pno_energy, occ_energy, fit_offset
        ),
        lambda: (amplitude, energy[0, :pairs]),
    )


def solution(mesh):
    return jax.shard_map(
        on_device,
        mesh=mesh,
        in_specs=(
            P(None, "orb", "aux", None),
            P(("aux", "orb"), None, None),
            P(("aux", "orb"), None),
            P(("aux", "orb"), None, None, None),
            P(("aux", "orb"), None, None),
            P(),
            P(),
        ),
        out_specs=(P(("aux", "orb"), None), P(("aux", "orb"))),
        check_vma=False,
    )
```
